32 devices in a mesh: pts: 4 (over y, core), ctr: 8 (over z, x).
Axes of the slice: x: 2, y: 2, z: 4, core: 2. Of those that a mesh axis runs over, the one named last changes fastest.
Arguments:
- points: bfloat16 [512, 512], P(('pts', 'ctr')), may hold values from -6 to 6
- point_class: int32 [512], P(('pts', 'ctr')), may hold values from 0 to 7
- targets: float32 [512, 128], P(('pts', 'ctr')), may hold values from -6 to 6
- class_weight: float32 [8], replicated, may hold values from 0.25 to 4
- inv_scale: float32 [512], replicated, may hold values from 0.003 to 0.3
- centers: bfloat16 [32768, 512], P('ctr'), may hold values from -6 to 6
- coefficients: bfloat16 [32768, 128], P('ctr'), may hold values from -2.5 to 2.5
- center_index: int32 [4096], replicated, may hold values from 0 to 32767, as said below
- factor: float32 [4096, 4096], P('ctr'), as said below
- panel_inverse: float32 [4096, 2048], P('ctr'), as said below
Outputs:
- gradient: float32 [32768, 128], P('ctr', 'pts')
- solved: float32 [4096, 128], P('ctr', 'pts')
The draws below stay inside these ranges and needn't reach their ends.
Inputs may be any that keep to these rules, and one draw needn't show every extreme that they name: `center_index`: the values are distinct; window row r lies in the center shard (index of ctr, 4096 centers each) numbered order[r mod 8] for one permutation order of the shards, so each shard holds exactly 512 window rows and the 512 rows of each aligned block of the window hold at most 64 of one shard's centers, a bound that is reached. factor is lower triangular with its diagonal between 1 and 2. `panel_inverse`: the rows of panel p hold the inverse of factor's diagonal block of rows and columns p * 2048 to (p + 1) * 2048 - 1.
All inputs are finite; a program needn't handle non-finite values.
Results may differ from the reference program's by a relative error of at most 0.0055.
Values may be sent and summed in bfloat16 or wider, within the bound.
A program may use at most 64 MiB of HBM per device.

```python
import math
import jax
import jax.numpy as jnp
from jax import lax

D = 512
TARGETS = 128
CLASSES = 8
CTR_DEV = 4096
PANEL = 2048
PANELS = 2
NPTS = 512
CENTERS = 32768
WIN = 4096
N_CTR = 8


def factor_matrix(key):
    folded = jax.random.fold_in(key, 11)
    strict_key, diagonal_key = jax.random.split(folded)
    strict = jnp.tril(jax.random.normal(strict_key, (WIN, WIN), jnp.float32), -1) * (0.6 / math.sqrt(WIN))
    diagonal = jax.random.uniform(diagonal_key, (WIN,), jnp.float32, 1.0, 2.0)
    return strict + jnp.diag(diagonal)


def draw_factor(key, part):
    return factor_matrix(key)


def draw_panel_inverse(key, part):
    matrix = factor_matrix(key)
    identity = jnp.eye(PANEL, dtype=jnp.float32)
    blocks = []
    for current in range(PANELS):
        begin = current * PANEL
        diagonal_block = matrix[begin:begin + PANEL, begin:begin + PANEL]
        blocks.append(jax.scipy.linalg.solve_triangular(diagonal_block, identity, lower=True))
    return jnp.concatenate(blocks, axis=0)


def draw_center_index(key, part):
    folded = jax.random.fold_in(key, 5)
    order_key, offset_key = jax.random.split(folded)
    shard_order = jax.random.permutation(order_key, N_CTR).astype(jnp.int32)
    rows = jnp.arange(WIN, dtype=jnp.int32)
    shard = shard_order[rows % N_CTR]
    occurrence = rows // N_CTR
    offset_keys = jax.random.split(offset_key, N_CTR)
    offsets = jax.vmap(lambda single: jax.random.permutation(single, CTR_DEV).astype(jnp.int32))(offset_keys)
    return (shard * CTR_DEV + offsets[shard, occurrence]).astype(jnp.int32)


def set_ends(drawn, key, least, top_value):
    spot = [jax.random.randint(jax.random.fold_in(key, axis), (), 0, length) for axis, length in enumerate(drawn.shape)]
    main_axis = drawn.shape.index(max(drawn.shape))
    beside = spot[:main_axis] + [(spot[main_axis] + 1) % drawn.shape[main_axis]] + spot[main_axis + 1:]
    return drawn.at[tuple(spot)].set(least).at[tuple(beside)].set(top_value)


def shard_levels(rng, dims, pieces, smallest, top_value):
    level = 1.0
    for position, parts in pieces:
        draws = jax.random.uniform(jax.random.fold_in(jax.random.fold_in(rng, 6), position), (parts,), jnp.float32, smallest / len(pieces), top_value / len(pieces))
        level = level * jnp.repeat(jnp.exp(draws), dims[position] // parts).reshape((-1,) + (1,) * (len(dims) - 1 - position))
    return level


def noise(key, shape, scale, most, pieces=(), held_as=jnp.bfloat16):
    gain = shard_levels(key, shape, pieces, -0.22, 0.18) if pieces else 1.0
    entries = jax.random.normal(key, shape, jnp.float32) * scale * gain
    return jnp.minimum(jnp.maximum(entries, -most), most).astype(held_as)


def setup_inputs(seed: int = 0) -> dict:
    streams_of = jax.random.split(jax.random.key(seed), 11)
    points = noise(streams_of[0], (NPTS, D), 1.0, 6.0, ((0, 32),))
    point_class = set_ends(jax.random.randint(streams_of[1], (NPTS,), 0, CLASSES), jax.random.fold_in(streams_of[1], 1), 0, CLASSES - 1).astype(jnp.int32)
    targets = noise(streams_of[2], (NPTS, TARGETS), 1.0, 6.0, ((0, 32),), jnp.float32)
    class_weight = jnp.clip(jnp.exp(jax.random.uniform(streams_of[3], (CLASSES,), jnp.float32, math.log(0.25), math.log(4.0))), 0.25, 4.0)
    inv_scale = jnp.clip(jnp.exp(jax.random.uniform(streams_of[4], (D,), jnp.float32, math.log(0.003), math.log(0.3))), 0.003, 0.3)
    centers = noise(streams_of[5], (CENTERS, D), 1.0, 6.0, ((0, 8),))
    coefficients = noise(streams_of[6], (CENTERS, TARGETS), 0.35, 2.5, ((0, 8),))
    center_index = draw_center_index(jax.random.fold_in(streams_of[10], 71), 0)
    factor = draw_factor(jax.random.fold_in(streams_of[10], 71), 0)
    panel_inverse = draw_panel_inverse(jax.random.fold_in(streams_of[10], 71), 0)
    return dict(points=points, point_class=point_class, targets=targets, class_weight=class_weight, inv_scale=inv_scale, centers=centers, coefficients=coefficients, center_index=center_index, factor=factor, panel_inverse=panel_inverse)


def gaussian(samples, anchors):
    products = lax.dot_general(samples.astype(jnp.float32), anchors.astype(jnp.float32), (((1,), (1,)), ((), ())), preferred_element_type=jnp.float32)
    left_norm = jnp.sum(jnp.square(samples.astype(jnp.float32)), axis=1)
    right_norm = jnp.sum(jnp.square(anchors.astype(jnp.float32)), axis=1)
    exponent = products - 0.5 * left_norm[:, None] - 0.5 * right_norm[None, :]
    return jnp.exp(exponent).astype(jnp.bfloat16)

def class_lookup(labels, table):
    classes = jnp.arange(table.shape[0], dtype=jnp.int32)
    return jnp.sum(jnp.where(labels[:, None] == classes[None, :], table[None, :], 0.0), axis=1)

def reference(points, point_class, targets, class_weight, inv_scale, centers, coefficients, center_index, factor, panel_inverse):
    scaled_points = (points.astype(jnp.float32) * inv_scale[None, :]).astype(jnp.bfloat16)
    scaled_centers = (centers.astype(jnp.float32) * inv_scale[None, :]).astype(jnp.bfloat16)
    center_blocks = scaled_centers.reshape(N_CTR, CTR_DEV, D)
    coef_blocks = coefficients.reshape(N_CTR, CTR_DEV, TARGETS)

    def accumulate(running, inputs):
        center_block, coef_block = inputs
        kernel = gaussian(scaled_points, center_block)
        return (running + jnp.dot(kernel.astype(jnp.float32), coef_block.astype(jnp.float32), preferred_element_type=jnp.float32), None)
    predicted, unused = lax.scan(accumulate, jnp.zeros((NPTS, TARGETS), jnp.float32), (center_blocks, coef_blocks))
    weight = class_lookup(point_class, class_weight)
    residual = (weight[:, None] * (predicted - targets)).astype(jnp.bfloat16)

    def backward(center_block):
        kernel = gaussian(scaled_points, center_block)
        return lax.dot_general(kernel.astype(jnp.float32), residual.astype(jnp.float32), (((0,), (0,)), ((), ())), preferred_element_type=jnp.float32)
    gradient = lax.map(backward, center_blocks).reshape(CENTERS, TARGETS)
    window = gradient[center_index]
    solved_full = jnp.zeros((WIN, TARGETS), jnp.float32)
    for current in range(PANELS):
        begin = current * PANEL
        rhs_part = window[begin:begin + PANEL]
        if current > 0:
            rhs_part = rhs_part - jnp.dot(factor[begin:begin + PANEL], solved_full, precision=lax.Precision.HIGHEST)
        panel_part = jnp.dot(panel_inverse[begin:begin + PANEL], rhs_part, precision=lax.Precision.HIGHEST)
        solved_full = solved_full.at[begin:begin + PANEL].set(panel_part)
    return (gradient, solved_full)
```

```python
import functools

import jax
import jax.numpy as jnp
from jax import lax
from jax.experimental import pallas as pl
from jax.experimental.pallas import tpu as pltpu
from jax.sharding import PartitionSpec as P

MESH = pl.DeviceIdType.MESH
NT = (((1,), (1,)), ((), ()))
F32 = jnp.float32
BF16 = jnp.bfloat16


def dot_nt(left, right):
    return lax.dot_general(left, right, NT, preferred_element_type=F32)


def kernel(
    n_pts, n_ctr, panels, chunk,
    pts_ref, cls_ref, tgt_ref, cw_ref, inv_ref, idx_ref, idx_hbm, cen_hbm, coef_hbm, fac_hbm, pinv_hbm,
    grad_ref, sol_ref,
    cen, coef, pinv_raw, pinv, fac_raw, fac, rnorm, pall, kmat, ksel,
    head, sel, part, part_recv, rall, wsend, wrecv, wpack, wblk, solsend, solrecv, rhssend, rhsrecv,
    loc, pt_s, pt_r, fw_s, fw_r, pr_s, pr_r, rs_s, rs_r, w_s, w_r, so_s, so_r, rh_s, rh_r,
):
    p_me, c_me = lax.axis_index("pts"), lax.axis_index("ctr")
    rows = pts_ref.shape[0]
    group = rows * n_ctr
    centers = cen.shape[0]
    feats = cen.shape[1]
    targets = tgt_ref.shape[1]
    tcols = targets // n_pts
    own_rows = pinv.shape[0]
    panel_rows = pinv.shape[1]
    owners = panel_rows // own_rows
    my_panel = c_me // owners
    chunks = centers // chunk

    def remote(src, dst, send, recv, p, c):
        return pltpu.make_async_remote_copy(
            src_ref=src, dst_ref=dst, send_sem=send, recv_sem=recv,
            device_id={"pts": p, "ctr": c}, device_id_type=MESH,
        )

    def each(n, fn):
        def step(k, carry):
            fn(k)
            return carry
        lax.fori_loop(0, n, step, 0)

    barrier = pltpu.get_barrier_semaphore()
    everyone = n_pts * n_ctr
    me = p_me * n_ctr + c_me

    def greet(k):
        other = lax.rem(me + k + 1, everyone)
        pl.semaphore_signal(
            barrier, inc=1,
            device_id={"pts": other // n_ctr, "ctr": lax.rem(other, n_ctr)}, device_id_type=MESH,
        )
    cen_copy = pltpu.make_async_copy(cen_hbm, cen, loc.at[0])
    coef_copy = pltpu.make_async_copy(coef_hbm, coef, loc.at[1])
    pinv_copy = pltpu.make_async_copy(pinv_hbm, pinv_raw, loc.at[2])
    fac_copy = pltpu.make_async_copy(fac_hbm.at[:, pl.ds(0, fac.shape[1])], fac_raw, loc.at[3])
    head_copy = pltpu.make_async_copy(idx_hbm.at[pl.ds(0, head.shape[0])], head, loc.at[4])
    cen_copy.start()
    each(everyone - 1, greet)
    coef_copy.start()

    inv = inv_ref[...]
    own_slot = pl.ds(pl.multiple_of(me * rows, rows), rows)
    pall[own_slot, :] = (pts_ref[...].astype(F32) * inv).astype(BF16)
    pl.semaphore_wait(barrier, everyone - 1)

    def pt_copy(c_src, c_dst):
        slot = pl.ds(pl.multiple_of((p_me * n_ctr + c_src) * rows, rows), rows)
        return remote(pall.at[slot], pall.at[slot], pt_s.at[c_dst], pt_r.at[c_src], p_me, c_dst)

    def peer(k):
        return lax.rem(c_me + k + 1, n_ctr)
    each(n_ctr - 1, lambda k: pt_copy(c_me, peer(k)).start())

    ones = jnp.ones((8, feats), BF16)
    cen_copy.wait()

    def scale(k):
        at = pl.ds(pl.multiple_of(k * chunk, chunk), chunk)
        scaled = (cen[at, :].astype(F32) * inv).astype(BF16)
        cen[at, :] = scaled
        square = jnp.square(scaled.astype(F32))
        high = square.astype(BF16)
        low = (square - high.astype(F32)).astype(BF16)
        rnorm[:, at] = 0.5 * (dot_nt(ones, high) + dot_nt(ones, low))
    each(chunks, scale)
    coef_copy.wait()
    pinv_copy.start()
    fac_copy.start()
    head_copy.start()

    each(n_ctr - 1, lambda k: pt_copy(peer(k), peer(k)).wait_recv())

    def group_at(p):
        return pl.ds(pl.multiple_of(p * group, group), group)

    def fw_copy(p_src, p_dst):
        at = group_at(p_src)
        return remote(pall.at[at], pall.at[at], fw_s.at[p_dst], fw_r.at[p_src], p_dst, c_me)

    pair = p_me // 2 * 2

    def mate(k):
        return 2 * pair + 1 - p_me if k == 0 else lax.rem(pair + k + 1, n_pts)
    for k in range(n_pts - 1):
        fw_copy(p_me, mate(k)).start()

    def half_norm(x):
        return 0.5 * jnp.sum(jnp.square(x.astype(F32)), axis=1, keepdims=True)

    def kernel_block(p, k):
        at = pl.ds(pl.multiple_of(k * chunk, chunk), chunk)
        mine = pall[group_at(p), :]
        exponent = dot_nt(mine, cen[at, :]) - half_norm(mine) - rnorm[0:1, at]
        block = jnp.exp(exponent).astype(BF16)
        kmat[group_at(p), at] = block
        return block, at

    def forward(k, total):
        block, at = kernel_block(p_me, k)
        return total + jnp.dot(block, coef[at, :], preferred_element_type=F32)
    total = lax.fori_loop(0, chunks, forward, jnp.zeros((group, targets), F32))
    part[...] = total.reshape(n_ctr, rows, targets)

    def pr_copy(c_src, c_dst):
        return remote(part.at[c_dst], part_recv.at[c_src], pr_s.at[c_dst], pr_r.at[c_src], p_me, c_dst)
    each(n_ctr - 1, lambda k: pr_copy(c_me, peer(k)).start())

    shift, wide_lanes = 64, idx_ref.shape[1]
    per = wide_lanes // n_ctr
    slots = sel.shape[0]
    relative = idx_ref[...] - c_me * centers
    relative = jnp.where((relative >= 0) & (relative < centers), relative, 0)

    def iota(shape, dim):
        return lax.broadcasted_iota(jnp.int32, shape, dim)

    def hot(mask):
        return jnp.where(mask, 1.0, 0.0).astype(BF16)
    fold = hot(iota((wide_lanes, wide_lanes), 0) // n_ctr == iota((wide_lanes, wide_lanes), 1))
    spread = hot(iota((slots, relative.shape[0]), 0) // per == iota((slots, relative.shape[0]), 1))

    def column(value):
        folded = jnp.dot(value.astype(F32).astype(BF16), fold, preferred_element_type=F32)
        return jnp.dot(spread, folded.astype(BF16), preferred_element_type=F32)
    both = shift * column(relative // shift) + column(lax.rem(relative, shift))
    at_lane = lax.rem(iota((slots, wide_lanes), 0), per) == iota((slots, wide_lanes), 1)
    local_row = jnp.sum(jnp.where(at_lane, both, 0.0), axis=1, keepdims=True).astype(jnp.int32)
    sel[...] = jnp.zeros_like(sel)

    def select(k):
        at = pl.ds(pl.multiple_of(k * chunk, chunk), chunk)
        picked = hot(iota((slots, chunk), 1) == local_row - k * chunk)
        sel[...] += jnp.dot(picked, cen[at, :], preferred_element_type=F32)
    each(chunks, select)

    each(n_ctr - 1, lambda k: pr_copy(peer(k), peer(k)).wait_recv())
    part_recv[c_me] = part[c_me]
    predicted = jnp.sum(part_recv[...], axis=0)
    same = iota((rows, rows), 0) == iota((rows, rows), 1)
    own_class = jnp.sum(jnp.where(same, cls_ref[...], 0), axis=1, keepdims=True)
    classes = lax.broadcasted_iota(jnp.int32, (rows, cw_ref.shape[1]), 1)
    weight = jnp.sum(jnp.where(own_class == classes, cw_ref[...], 0.0), axis=1, keepdims=True)
    rall[own_slot, :] = (weight * (predicted - tgt_ref[...])).astype(BF16)

    def rs_copy(src, dst):
        slot = pl.ds(pl.multiple_of(src * rows, rows), rows)
        return remote(
            rall.at[slot], rall.at[slot], rs_s.at[dst], rs_r.at[src], dst // n_ctr, lax.rem(dst, n_ctr)
        )

    def other(k):
        return lax.rem(me + k + 1, everyone)
    each(everyone - 1, lambda k: rs_copy(me, other(k)).start())

    for k in range(n_pts - 1):
        fw_copy(mate(k), mate(k)).wait_recv()
        each(chunks, functools.partial(kernel_block, mate(k)))

    chosen = sel[...].astype(BF16)
    chosen_norm = half_norm(chosen)

    def window_kernel(p):
        mine = pall[group_at(p), :]
        square = jnp.square(mine.astype(F32))
        high = square.astype(BF16)
        low = (square - high.astype(F32)).astype(BF16)
        norm = 0.5 * (dot_nt(ones, high) + dot_nt(ones, low))
        ksel[:, group_at(p)] = jnp.exp(dot_nt(chosen, mine) - norm[0:1] - chosen_norm).astype(BF16)
    each(n_pts, window_kernel)

    each(everyone - 1, lambda k: rs_copy(other(k), other(k)).wait_recv())

    source = lax.broadcasted_iota(jnp.int32, (targets, targets), 0)
    lane = lax.broadcasted_iota(jnp.int32, (targets, targets), 1)
    pick = (source == p_me * tcols + lax.rem(lane, tcols)).astype(BF16)
    wide = jnp.dot(rall[...], pick, preferred_element_type=F32).astype(BF16)
    window = jnp.dot(ksel[...], wide, preferred_element_type=F32)
    run = wsend.shape[1]
    lane_group = lax.broadcasted_iota(jnp.int32, (run, targets), 1) // tcols
    for panel in range(panels):
        packed = jnp.zeros((run, targets), F32)
        for g in range(n_pts):
            begin = (panel * n_pts + g) * run
            packed = packed + jnp.where(lane_group == g, window[begin:begin + run], 0.0)
        wsend[panel] = packed.astype(BF16)

    def w_copy(c_src, c_dst):
        return remote(
            wsend.at[c_dst // owners], wrecv.at[c_src], w_s.at[c_dst], w_r.at[c_src], p_me, c_dst
        )
    each(n_ctr - 1, lambda k: w_copy(c_me, peer(k)).start())
    wrecv[c_me] = wsend[my_panel]

    tall = lax.broadcasted_iota(jnp.int32, (tcols, targets), 1)
    first = lax.broadcasted_iota(jnp.int32, (tcols, targets), 0)
    pick_t = (tall == p_me * tcols + first).astype(BF16)
    wide_t = dot_nt(pick_t, rall[...]).astype(BF16)

    def backward(k):
        at = pl.ds(pl.multiple_of(k * chunk, chunk), chunk)
        grad_ref[:, at] = jnp.dot(wide_t, kmat[:, at], preferred_element_type=F32)
    each(chunks, backward)
    pinv_copy.wait()
    fac_copy.wait()
    head_copy.wait()
    pinv[...] = pinv_raw[...].astype(BF16)

    each(n_ctr - 1, lambda k: w_copy(peer(k), peer(k)).wait_recv())
    for o in range(n_ctr):
        wpack[pl.ds(o, run, stride=n_ctr), :] = wrecv[head[o // wide_lanes, o % wide_lanes] // centers].astype(F32)

    def so_copy(c_src, c_dst):
        return remote(solsend, solrecv.at[c_src], so_s.at[c_dst], so_r.at[c_src], p_me, c_dst)

    def rh_copy(c_src, c_dst):
        at = lax.rem(c_src, owners)
        return remote(rhssend, rhsrecv.at[at], rh_s.at[c_dst], rh_r.at[at], p_me, c_dst)

    for panel in range(panels):
        @pl.when(my_panel == panel)
        def _():
            if panel == 0:
                turned = wpack[...].T.astype(BF16)
                rhs = jnp.concatenate([turned[g * tcols:(g + 1) * tcols] for g in range(n_pts)], axis=1)
            else:
                local = (c_me - panel * owners) * own_rows
                part_len = panel_rows // n_pts
                within = pl.multiple_of(lax.rem(local, part_len), own_rows)
                turned = wpack[pl.ds(within, own_rows), :].T
                for g in range(n_pts):
                    wblk[g] = turned[g * tcols:(g + 1) * tcols]
                own = wblk[local // part_len]
                done = panel * owners
                fac[...] = fac_raw[...].astype(BF16)
                each(done, lambda k: so_copy(k, k).wait_recv())
                solved = jnp.concatenate([solrecv[b] for b in range(done)], axis=1)
                own = own - dot_nt(solved, fac[:, :done * own_rows])
                rhssend[...] = own.astype(BF16)

                def fellow(k):
                    return panel * owners + lax.rem(c_me - panel * owners + k + 1, owners)
                each(owners - 1, lambda k: rh_copy(c_me, fellow(k)).start())
                rhsrecv[c_me - panel * owners] = rhssend[...]
                each(owners - 1, lambda k: rh_copy(fellow(k), fellow(k)).wait_recv())
                rhs = jnp.concatenate([rhsrecv[b] for b in range(owners)], axis=1)
            result = dot_nt(rhs, pinv[...])
            sol_ref[...] = result
            later = (panels - 1 - panel) * owners
            if later:
                solsend[...] = result.astype(BF16)

                def after(k):
                    return (panel + 1) * owners + lax.rem(k + c_me, later)
                each(later, lambda k: so_copy(c_me, after(k)).start())
                each(later, lambda k: so_copy(c_me, after(k)).wait_send())
            if panel > 0:
                each(owners - 1, lambda k: rh_copy(c_me, fellow(k)).wait_send())

    each(n_ctr - 1, lambda k: pt_copy(c_me, peer(k)).wait_send())
    for k in range(n_pts - 1):
        fw_copy(p_me, mate(k)).wait_send()
    each(n_ctr - 1, lambda k: pr_copy(c_me, peer(k)).wait_send())
    each(everyone - 1, lambda k: rs_copy(me, other(k)).wait_send())
    each(n_ctr - 1, lambda k: w_copy(c_me, peer(k)).wait_send())


def emit(grad_ref, sol_ref, grad_out, sol_out, sem):
    first = pltpu.make_async_copy(grad_ref, grad_out, sem.at[0])
    second = pltpu.make_async_copy(sol_ref, sol_out, sem.at[1])
    first.start()
    second.start()
    first.wait()
    second.wait()


def body(
    points, point_class, targets, class_weight, inv_scale, centers, coefficients, center_index, factor, panel_inverse
):
    n_pts, n_ctr = lax.axis_size("pts"), lax.axis_size("ctr")
    rows, feats = points.shape
    n_cen, n_tgt = coefficients.shape
    tcols = n_tgt // n_pts
    own_rows, panel_rows = panel_inverse.shape
    panels = factor.shape[1] // panel_rows
    owners = panel_rows // own_rows
    everyone = n_pts * n_ctr
    total = rows * everyone
    slots = center_index.shape[0] // n_ctr
    run = slots // panels // n_pts
    solved_cols = panel_rows * (panels - 1)
    index = center_index.reshape(-1, 128)
    vmem = pl.BlockSpec(memory_space=pltpu.VMEM)
    hbm = pl.BlockSpec(memory_space=pltpu.HBM)
    dma = pltpu.SemaphoreType.DMA
    scratch = [
        pltpu.VMEM((n_cen, feats), BF16),
        pltpu.VMEM((n_cen, n_tgt), BF16),
        pltpu.VMEM((own_rows, panel_rows), F32),
        pltpu.VMEM((own_rows, panel_rows), BF16),
        pltpu.VMEM((own_rows, solved_cols), F32),
        pltpu.VMEM((own_rows, solved_cols), BF16),
        pltpu.VMEM((8, n_cen), F32),
        pltpu.VMEM((total, feats), BF16),
        pltpu.VMEM((total, n_cen), BF16),
        pltpu.VMEM((slots, total), BF16),
        pltpu.SMEM((8, 128), jnp.int32),
        pltpu.VMEM((slots, feats), F32),
        pltpu.VMEM((n_ctr, rows, n_tgt), F32),
        pltpu.VMEM((n_ctr, rows, n_tgt), F32),
        pltpu.VMEM((total, n_tgt), BF16),
        pltpu.VMEM((panels, run, n_tgt), BF16),
        pltpu.VMEM((n_ctr, run, n_tgt), BF16),
        pltpu.VMEM((run * n_ctr, n_tgt), F32),
        pltpu.VMEM((n_pts, tcols, own_rows), F32),
        pltpu.VMEM((tcols, own_rows), BF16),
        pltpu.VMEM((owners * (panels - 1), tcols, own_rows), BF16),
        pltpu.VMEM((tcols, own_rows), BF16),
        pltpu.VMEM((owners, tcols, own_rows), BF16),
        dma((5,)),
        dma((n_ctr,)), dma((n_ctr,)),
        dma((n_pts,)), dma((n_pts,)),
        dma((n_ctr,)), dma((n_ctr,)),
        dma((everyone,)), dma((everyone,)),
        dma((n_ctr,)), dma((n_ctr,)),
        dma((n_ctr,)), dma((n_ctr,)),
        dma((n_ctr,)), dma((owners,)),
    ]
    grad, solved = pl.pallas_call(
        functools.partial(kernel, n_pts, n_ctr, panels, 1024),
        out_shape=(
            pltpu.VMEM((tcols, n_cen), F32),
            pltpu.VMEM((tcols, own_rows), F32),
        ),
        in_specs=[vmem] * 6 + [hbm] * 5,
        out_specs=(vmem, vmem),
        scratch_shapes=scratch,
        compiler_params=pltpu.CompilerParams(
            collective_id=0, has_side_effects=True, vmem_limit_bytes=60000000
        ),
        name="falkon",
    )(
        points, point_class[None, :], targets, class_weight[None, :], inv_scale[None, :],
        index, index, centers, coefficients, factor, panel_inverse,
    )
    grad, solved = pl.pallas_call(
        emit,
        out_shape=(
            jax.ShapeDtypeStruct((tcols, n_cen), F32),
            jax.ShapeDtypeStruct((tcols, own_rows), F32),
        ),
        in_specs=[vmem, vmem],
        out_specs=(hbm, hbm),
        scratch_shapes=[dma((2,))],
        compiler_params=pltpu.CompilerParams(vmem_limit_bytes=1048576),
        name="emit",
    )(grad, solved)
    return grad.T, solved.T


def solution(mesh):
    placed = (
        P(("pts", "ctr"), None),
        P(("pts", "ctr")),
        P(("pts", "ctr"), None),
        P(),
        P(),
        P("ctr", None),
        P("ctr", None),
        P(),
        P("ctr", None),
        P("ctr", None),
    )
    return jax.shard_map(
        body,
        mesh=mesh,
        in_specs=placed,
        out_specs=(P("ctr", "pts"), P("ctr", "pts")),
        check_vma=False,
    )
```

```python
import functools

import jax
import jax.numpy as jnp
from jax import lax
from jax.experimental import pallas as pl
from jax.experimental.pallas import tpu as pltpu
from jax.sharding import PartitionSpec as P

MESH = pl.DeviceIdType.MESH
NT = (((1,), (1,)), ((), ()))
F32 = jnp.float32
BF16 = jnp.bfloat16
LANES = 128


def dot_nt(left, right):
    return lax.dot_general(left, right, NT, preferred_element_type=F32)


def iota(shape, dim):
    return lax.broadcasted_iota(jnp.int32, shape, dim)


def hot(mask):
    return jnp.where(mask, 1.0, 0.0).astype(BF16)


def half_norm(x):
    return 0.5 * jnp.sum(jnp.square(x.astype(F32)), axis=1, keepdims=True)


def half_norm_row(x):
    square = jnp.square(x.astype(F32))
    folded = square[:, :LANES]
    for begin in range(LANES, square.shape[1], LANES):
        folded = folded + square[:, begin:begin + LANES]
    return 0.5 * jnp.sum(folded.T, axis=0, keepdims=True)


def each(n, fn):
    def step(k, carry):
        fn(k)
        return carry
    lax.fori_loop(0, n, step, 0)


def kernel(
    n_pts, n_ctr, panels, chunk, sub,
    pts_hbm, cls_hbm, tgt_hbm, cw_hbm, inv_hbm, idx_hbm, cen_hbm, coef_hbm, fac_hbm, pinv_hbm,
    grad_ref, sol_ref,
    pts, cls, tgt, cw, inv_row, idx, head,
    cen, coef, pinv_raw, pinv, fac_raw, fac, rnorm, pnorm, pall, kmat, ksel,
    sel, total_acc, part, part_recv, wt_send, wt_recv, rsend, rbuf,
    wsend, wrecv, wpack, wblk, solsend, solrecv, rhssend, rhsrecv,
    loc, cen_sem, pt_s, pt_r, fw_s, fw_r, pr_s, pr_r, wt_s, wt_r, rs_s, rs_r, w_s, w_r, so_s, so_r, rh_s, rh_r,
):
    p_me, c_me = lax.axis_index("pts"), lax.axis_index("ctr")
    rows, feats = pts.shape
    group = rows * n_ctr
    centers = cen.shape[0]
    targets = tgt.shape[1]
    tcols = targets // n_pts
    own_rows, panel_rows = pinv.shape
    owners = panel_rows // own_rows
    my_panel = c_me // owners
    chunks = centers // chunk
    blocks = rbuf.shape[0]
    pt_blocks = blocks // n_pts
    per_block = n_ctr // pt_blocks
    copies = n_ctr // blocks
    width = rows * per_block
    me = p_me * n_ctr + c_me
    blk = lax.rem(c_me, blocks)
    rep = c_me // blocks
    blk_pts = lax.rem(blk, n_pts)
    own_block = blk_pts == p_me

    def remote(src, dst, send, recv, p, c):
        return pltpu.make_async_remote_copy(
            src_ref=src, dst_ref=dst, send_sem=send, recv_sem=recv,
            device_id={"pts": p, "ctr": c}, device_id_type=MESH,
        )

    def local(src, dst, k):
        return pltpu.make_async_copy(src, dst, loc.at[k])

    def cen_copy(k):
        at = pl.ds(pl.multiple_of(k * chunk, chunk), chunk)
        return pltpu.make_async_copy(cen_hbm.at[at], cen.at[at], cen_sem.at[k])

    pts_copy = local(pts_hbm, pts, 0)
    inv_copy = local(inv_hbm, inv_row, 1)
    cls_copy = local(cls_hbm, cls, 2)
    cw_copy = local(cw_hbm, cw, 3)
    tgt_copy = local(tgt_hbm, tgt, 4)
    idx_copy = local(idx_hbm, idx, 5)
    head_copy = local(idx_hbm.at[pl.ds(0, head.shape[0])], head, 6)
    coef_copy = local(coef_hbm, coef, 7)
    pinv_copy = local(pinv_hbm, pinv_raw, 8)
    fac_copy = local(fac_hbm.at[:, pl.ds(0, fac.shape[1])], fac_raw, 9)
    pts_copy.start()
    inv_copy.start()

    barrier = pltpu.get_barrier_semaphore()

    def peer(k):
        return lax.rem(c_me + k + 1, n_ctr)
    pair = p_me // 2 * 2

    def mate(k):
        return 2 * pair + 1 - p_me if k == 0 else lax.rem(pair + k + 1, n_pts)

    def source(k):
        p = lax.rem(p_me + k, n_pts)
        b = lax.rem(blk // n_pts + k // n_pts, pt_blocks)
        return p, b, rep * blocks + b * n_pts + p_me

    def greet(p, c):
        pl.semaphore_signal(barrier, inc=1, device_id={"pts": p, "ctr": c}, device_id_type=MESH)

    def foreign(k):
        return jnp.logical_or(k != 0, jnp.logical_not(own_block))

    each(n_ctr - 1, lambda k: greet(p_me, peer(k)))
    for k in range(n_pts - 1):
        greet(mate(k), c_me)

    def greet_source(k):
        @pl.when(foreign(k))
        def _():
            p, _, c = source(k)
            greet(p, c)
    each(blocks, greet_source)
    cls_copy.start()
    cw_copy.start()
    each(chunks, lambda k: cen_copy(k).start())
    idx_copy.start()
    tgt_copy.start()
    head_copy.start()
    coef_copy.start()

    pts_copy.wait()
    inv_copy.wait()
    inv = inv_row[...]
    own_slot = pl.ds(pl.multiple_of(me * rows, rows), rows)
    pall[own_slot, :] = (pts[...].astype(F32) * inv).astype(BF16)
    pl.semaphore_wait(barrier, n_ctr + n_pts - 2 + blocks - own_block.astype(jnp.int32))

    def pt_copy(c_src, c_dst):
        slot = pl.ds(pl.multiple_of((p_me * n_ctr + c_src) * rows, rows), rows)
        return remote(pall.at[slot], pall.at[slot], pt_s.at[c_dst], pt_r.at[c_src], p_me, c_dst)
    each(n_ctr - 1, lambda k: pt_copy(c_me, peer(k)).start())

    cls_copy.wait()
    cw_copy.wait()
    lane_of = lax.rem(c_me, per_block) * rows
    place = hot(iota((rows, width), 1) == iota((rows, width), 0) + lane_of)
    label = jnp.dot(
        jnp.broadcast_to(cls[...].astype(F32).astype(BF16), (8, rows)), place, preferred_element_type=F32
    )
    mine_lane = (iota((8, width), 1) >= lane_of) & (iota((8, width), 1) < lane_of + rows)
    weight = jnp.zeros((8, width), F32)
    for k in range(cw.shape[1]):
        weight = jnp.where(mine_lane & (label == float(k)), cw[0, k], weight)
    wt_send[...] = weight

    def wt_dest(k):
        turn = lax.rem(c_me + k, per_block)
        return turn // n_pts * blocks + c_me // per_block * n_pts + lax.rem(turn, n_pts)

    def wt_src(k):
        return blk // n_pts * per_block + k

    def wt_copy(c_src, c_dst):
        at = lax.rem(c_src, per_block)
        return remote(wt_send, wt_recv.at[at], wt_s.at[c_dst], wt_r.at[at], p_me, c_dst)

    def not_me(c, fn):
        @pl.when(c != c_me)
        def _():
            fn(c)
    each(per_block, lambda k: not_me(wt_dest(k), lambda c: wt_copy(c_me, c).start()))

    @pl.when(c_me // per_block == blk // n_pts)
    def _():
        wt_recv[lax.rem(c_me, per_block)] = weight

    step = 256

    def scale(k):
        at = pl.ds(pl.multiple_of(k * step, step), step)
        scaled = (cen[at, :].astype(F32) * inv).astype(BF16)
        cen[at, :] = scaled
        rnorm[0:1, at] = half_norm_row(scaled)

    def scale_chunk(k):
        cen_copy(k).wait()
        each(chunk // step, lambda j: scale(k * (chunk // step) + j))
    each(chunks, scale_chunk)

    idx_copy.wait()
    shift, wide_lanes = 64, idx.shape[1]
    per = wide_lanes // n_ctr
    slots = sel.shape[0]
    relative = idx[...] - c_me * centers
    relative = jnp.where((relative >= 0) & (relative < centers), relative, 0)
    fold = hot(iota((wide_lanes, wide_lanes), 0) // n_ctr == iota((wide_lanes, wide_lanes), 1))
    spread = hot(iota((slots, relative.shape[0]), 0) // per == iota((slots, relative.shape[0]), 1))

    def column(value):
        folded = jnp.dot(value.astype(F32).astype(BF16), fold, preferred_element_type=F32)
        return jnp.dot(spread, folded.astype(BF16), preferred_element_type=F32)
    both = shift * column(relative // shift) + column(lax.rem(relative, shift))
    at_lane = lax.rem(iota((slots, wide_lanes), 0), per) == iota((slots, wide_lanes), 1)
    local_row = jnp.sum(jnp.where(at_lane, both, 0.0), axis=1, keepdims=True).astype(jnp.int32)
    coef_copy.wait()
    tgt_copy.wait()
    head_copy.wait()
    pinv_copy.start()
    fac_copy.start()

    each(n_ctr - 1, lambda k: pt_copy(peer(k), peer(k)).wait_recv())

    def group_at(p):
        return pl.ds(pl.multiple_of(p * group, group), group)

    def fw_copy(p_src, p_dst):
        at = group_at(p_src)
        return remote(pall.at[at], pall.at[at], fw_s.at[p_dst], fw_r.at[p_src], p_dst, c_me)
    for k in range(n_pts - 1):
        fw_copy(p_me, mate(k)).start()

    def sub_at(k, j):
        return pl.ds(pl.multiple_of(k * chunk + j * sub, sub), sub)

    def kernel_block(left, norm, at):
        return jnp.exp(dot_nt(left, cen[at, :]) - norm - rnorm[0:1, at]).astype(BF16)
    mine = pall[group_at(p_me), :]
    mine_norm = half_norm(mine)
    pnorm[group_at(p_me), :] = jnp.broadcast_to(mine_norm, (group, LANES))

    def forward(k, total):
        at = pl.ds(pl.multiple_of(k * chunk, chunk), chunk)
        block = kernel_block(mine, mine_norm, at)
        kmat[group_at(p_me), at] = block
        return total + jnp.dot(block, coef[at, :], preferred_element_type=F32)
    total = jnp.zeros((group, targets), F32)
    for k in range(chunks):
        total = forward(k, total)
    total_acc[...] = total
    own_rows_at = pl.ds(pl.multiple_of(c_me * rows, rows), rows)
    total_acc[own_rows_at, :] = total_acc[own_rows_at, :] - tgt[...]
    for b in range(pt_blocks):
        turned = total_acc[b * width:(b + 1) * width, :].T
        for q in range(n_pts):
            part[b * n_pts + q] = turned[q * tcols:(q + 1) * tcols]

    def pr_copy(c_src, c_dst):
        return remote(
            part.at[lax.rem(c_dst, blocks)], part_recv.at[c_src], pr_s.at[c_dst], pr_r.at[c_src], p_me, c_dst
        )
    each(n_ctr - 1, lambda k: pr_copy(c_me, peer(k)).start())
    part_recv[c_me] = part[blk]

    sel[...] = jnp.zeros_like(sel)

    def select(k):
        at = pl.ds(pl.multiple_of(k * chunk, chunk), chunk)
        picked = hot(iota((slots, chunk), 1) == local_row - k * chunk)
        sel[...] += jnp.dot(picked, cen[at, :], preferred_element_type=F32)
    each(chunks, select)

    each(per_block, lambda k: not_me(wt_src(k), lambda c: wt_copy(c, c).wait_recv()))
    weights = jnp.sum(wt_recv[...], axis=0)[0:1]
    each(n_ctr - 1, lambda k: pr_copy(peer(k), peer(k)).wait_recv())
    residual = (weights * jnp.sum(part_recv[...], axis=0)).astype(BF16)
    rsend[...] = residual

    def rs_slot(p, b):
        return p * pt_blocks + b

    def rs_copy(p_src, b_src, p_dst, c_dst):
        at = rs_slot(p_src, b_src)
        return remote(rsend, rbuf.at[at], rs_s.at[lax.rem(c_dst, blocks)], rs_r.at[at], p_dst, c_dst)

    def rs_out(k):
        return rs_copy(p_me, blk // n_pts, blk_pts, rep * blocks + lax.rem(blk + k, blocks))

    def rs_in(k):
        p, b, _ = source(k)
        return rs_copy(p, b, p_me, c_me)

    def rs_each(fn):
        def step(k):
            @pl.when(foreign(k))
            def _():
                fn(k)
        each(blocks, step)
    rs_each(lambda k: rs_out(k).start())

    @pl.when(own_block)
    def _():
        rbuf[rs_slot(p_me, blk // n_pts)] = residual

    for k in range(n_pts - 1):
        fw_copy(mate(k), mate(k)).wait_recv()
    together = n_pts - 1 if group * n_pts <= 512 else 1
    for first in range(0, n_pts - 1, together):
        mates = [mate(k) for k in range(first, first + together)]
        left = jnp.concatenate([pall[group_at(p), :] for p in mates], axis=0)
        left_norm = half_norm(left)
        for k, p in enumerate(mates):
            pnorm[group_at(p), :] = jnp.broadcast_to(left_norm[k * group:(k + 1) * group], (group, LANES))

        def fill(k):
            for j in range(chunk // sub):
                at = sub_at(k, j)
                block = kernel_block(left, left_norm, at)
                for n, p in enumerate(mates):
                    kmat[group_at(p), at] = block[n * group:(n + 1) * group]
        each(chunks, fill)

    chosen = sel[...].astype(BF16)
    chosen_norm = half_norm(chosen)
    span = 512

    def window_kernel(k):
        at = pl.ds(pl.multiple_of(k * span, span), span)
        norm = pnorm[at, :].T[0:1]
        ksel[:, at] = jnp.exp(dot_nt(chosen, pall[at, :]) - norm - chosen_norm).astype(BF16)
    each(pall.shape[0] // span, window_kernel)

    rs_each(lambda k: rs_in(k).wait_recv())

    wide_t = jnp.concatenate([rbuf[b] for b in range(blocks)], axis=1)
    window = dot_nt(ksel[...], jnp.concatenate([wide_t] * n_pts, axis=0))
    run = wsend.shape[1]
    lane_group = iota((run, targets), 1) // tcols
    for panel in range(panels):
        packed = jnp.zeros((run, targets), F32)
        for g in range(n_pts):
            begin = (panel * n_pts + g) * run
            packed = packed + jnp.where(lane_group == g, window[begin:begin + run], 0.0)
        wsend[panel] = packed.astype(BF16)

    def w_copy(c_src, c_dst):
        return remote(
            wsend.at[c_dst // owners], wrecv.at[c_src], w_s.at[c_dst], w_r.at[c_src], p_me, c_dst
        )
    each(n_ctr - 1, lambda k: w_copy(c_me, peer(k)).start())
    wrecv[c_me] = wsend[my_panel]

    def backward(k):
        at = pl.ds(pl.multiple_of(k * chunk, chunk), chunk)
        grad_ref[:, at] = jnp.dot(wide_t, kmat[:, at], preferred_element_type=F32)
    each(chunks, backward)
    pinv_copy.wait()
    fac_copy.wait()
    pinv[...] = pinv_raw[...].astype(BF16)

    each(n_ctr - 1, lambda k: pt_copy(c_me, peer(k)).wait_send())
    each(per_block, lambda k: not_me(wt_dest(k), lambda c: wt_copy(c_me, c).wait_send()))
    for k in range(n_pts - 1):
        fw_copy(p_me, mate(k)).wait_send()
    each(n_ctr - 1, lambda k: pr_copy(c_me, peer(k)).wait_send())
    rs_each(lambda k: rs_out(k).wait_send())

    each(n_ctr - 1, lambda k: w_copy(peer(k), peer(k)).wait_recv())
    for o in range(n_ctr):
        wpack[pl.ds(o, run, stride=n_ctr), :] = wrecv[head[o // wide_lanes, o % wide_lanes] // centers].astype(F32)

    def so_copy(c_src, c_dst):
        return remote(solsend, solrecv.at[c_src], so_s.at[c_dst], so_r.at[c_src], p_me, c_dst)

    def rh_copy(c_src, c_dst):
        at = lax.rem(c_src, owners)
        return remote(rhssend, rhsrecv.at[at], rh_s.at[c_dst], rh_r.at[at], p_me, c_dst)

    for panel in range(panels):
        @pl.when(my_panel == panel)
        def _():
            if panel == 0:
                turned = wpack[...].T.astype(BF16)
                rhs = jnp.concatenate([turned[g * tcols:(g + 1) * tcols] for g in range(n_pts)], axis=1)
            else:
                offset = (c_me - panel * owners) * own_rows
                part_len = panel_rows // n_pts
                within = pl.multiple_of(lax.rem(offset, part_len), own_rows)
                turned = wpack[pl.ds(within, own_rows), :].T
                for g in range(n_pts):
                    wblk[g] = turned[g * tcols:(g + 1) * tcols]
                own = wblk[offset // part_len]
                done = panel * owners
                fac[...] = fac_raw[...].astype(BF16)
                each(done, lambda k: so_copy(k, k).wait_recv())
                solved = jnp.concatenate([solrecv[b] for b in range(done)], axis=1)
                own = own - dot_nt(solved, fac[:, :done * own_rows])
                rhssend[...] = own.astype(BF16)

                def fellow(k):
                    return panel * owners + lax.rem(c_me - panel * owners + k + 1, owners)
                each(owners - 1, lambda k: rh_copy(c_me, fellow(k)).start())
                rhsrecv[c_me - panel * owners] = rhssend[...]
                each(owners - 1, lambda k: rh_copy(fellow(k), fellow(k)).wait_recv())
                rhs = jnp.concatenate([rhsrecv[b] for b in range(owners)], axis=1)
            result = dot_nt(rhs, pinv[...])
            sol_ref[...] = result
            later = (panels - 1 - panel) * owners
            if later:
                solsend[...] = result.astype(BF16)

                def after(k):
                    return (panel + 1) * owners + lax.rem(k + c_me, later)
                each(later, lambda k: so_copy(c_me, after(k)).start())
                each(later, lambda k: so_copy(c_me, after(k)).wait_send())
            if panel > 0:
                each(owners - 1, lambda k: rh_copy(c_me, fellow(k)).wait_send())

    each(n_ctr - 1, lambda k: w_copy(c_me, peer(k)).wait_send())


def emit(grad_ref, sol_ref, grad_out, sol_out, sem):
    first = pltpu.make_async_copy(grad_ref, grad_out, sem.at[0])
    second = pltpu.make_async_copy(sol_ref, sol_out, sem.at[1])
    first.start()
    second.start()
    first.wait()
    second.wait()


def body(
    points, point_class, targets, class_weight, inv_scale, centers, coefficients, center_index, factor, panel_inverse
):
    n_pts, n_ctr = lax.axis_size("pts"), lax.axis_size("ctr")
    rows, feats = points.shape
    n_cen, n_tgt = coefficients.shape
    tcols = n_tgt // n_pts
    own_rows, panel_rows = panel_inverse.shape
    panels = factor.shape[1] // panel_rows
    owners = panel_rows // own_rows
    total = rows * n_pts * n_ctr
    group = rows * n_ctr
    per_block = LANES // rows
    pt_blocks = n_ctr // per_block
    blocks = n_pts * pt_blocks
    slots = center_index.shape[0] // n_ctr
    run = slots // panels // n_pts
    solved_cols = panel_rows * (panels - 1)
    chunk = 1024
    index = center_index.reshape(-1, LANES)
    vmem = pl.BlockSpec(memory_space=pltpu.VMEM)
    hbm = pl.BlockSpec(memory_space=pltpu.HBM)
    dma = pltpu.SemaphoreType.DMA
    scratch = [
        pltpu.VMEM((rows, feats), BF16),
        pltpu.VMEM((1, rows), jnp.int32),
        pltpu.VMEM((rows, n_tgt), F32),
        pltpu.SMEM((1, class_weight.shape[0]), F32),
        pltpu.VMEM((1, feats), F32),
        pltpu.VMEM(index.shape, jnp.int32),
        pltpu.SMEM((8, LANES), jnp.int32),
        pltpu.VMEM((n_cen, feats), BF16),
        pltpu.VMEM((n_cen, n_tgt), BF16),
        pltpu.VMEM((own_rows, panel_rows), F32),
        pltpu.VMEM((own_rows, panel_rows), BF16),
        pltpu.VMEM((own_rows, solved_cols), F32),
        pltpu.VMEM((own_rows, solved_cols), BF16),
        pltpu.VMEM((8, n_cen), F32),
        pltpu.VMEM((total, LANES), F32),
        pltpu.VMEM((total, feats), BF16),
        pltpu.VMEM((total, n_cen), BF16),
        pltpu.VMEM((slots, total), BF16),
        pltpu.VMEM((slots, feats), F32),
        pltpu.VMEM((group, n_tgt), F32),
        pltpu.VMEM((blocks, tcols, LANES), F32),
        pltpu.VMEM((n_ctr, tcols, LANES), F32),
        pltpu.VMEM((8, LANES), F32),
        pltpu.VMEM((per_block, 8, LANES), F32),
        pltpu.VMEM((tcols, LANES), BF16),
        pltpu.VMEM((blocks, tcols, LANES), BF16),
        pltpu.VMEM((panels, run, n_tgt), BF16),
        pltpu.VMEM((n_ctr, run, n_tgt), BF16),
        pltpu.VMEM((run * n_ctr, n_tgt), F32),
        pltpu.VMEM((n_pts, tcols, own_rows), F32),
        pltpu.VMEM((tcols, own_rows), BF16),
        pltpu.VMEM((owners * (panels - 1), tcols, own_rows), BF16),
        pltpu.VMEM((tcols, own_rows), BF16),
        pltpu.VMEM((owners, tcols, own_rows), BF16),
        dma((10,)), dma((n_cen // chunk,)),
        dma((n_ctr,)), dma((n_ctr,)),
        dma((n_pts,)), dma((n_pts,)),
        dma((n_ctr,)), dma((n_ctr,)),
        dma((n_ctr,)), dma((per_block,)),
        dma((blocks,)), dma((blocks,)),
        dma((n_ctr,)), dma((n_ctr,)),
        dma((n_ctr,)), dma((n_ctr,)),
        dma((n_ctr,)), dma((owners,)),
    ]
    grad, solved = pl.pallas_call(
        functools.partial(kernel, n_pts, n_ctr, panels, chunk, 256),
        out_shape=(
            pltpu.VMEM((tcols, n_cen), F32),
            pltpu.VMEM((tcols, own_rows), F32),
        ),
        in_specs=[hbm] * 10,
        out_specs=(vmem, vmem),
        scratch_shapes=scratch,
        compiler_params=pltpu.CompilerParams(
            collective_id=0, has_side_effects=True, vmem_limit_bytes=60000000
        ),
        name="falkon",
    )(
        points, point_class[None, :], targets, class_weight[None, :], inv_scale[None, :],
        index, centers, coefficients, factor, panel_inverse,
    )
    grad, solved = pl.pallas_call(
        emit,
        out_shape=(
            jax.ShapeDtypeStruct((tcols, n_cen), F32),
            jax.ShapeDtypeStruct((tcols, own_rows), F32),
        ),
        in_specs=[vmem, vmem],
        out_specs=(hbm, hbm),
        scratch_shapes=[dma((2,))],
        compiler_params=pltpu.CompilerParams(vmem_limit_bytes=1048576),
        name="emit",
    )(grad, solved)
    return grad.T, solved.T


def solution(mesh):
    placed = (
        P(("pts", "ctr"), None),
        P(("pts", "ctr")),
        P(("pts", "ctr"), None),
        P(),
        P(),
        P("ctr", None),
        P("ctr", None),
        P(),
        P("ctr", None),
        P("ctr", None),
    )
    return jax.shard_map(
        body,
        mesh=mesh,
        in_specs=placed,
        out_specs=(P("ctr", "pts"), P("ctr", "pts")),
        check_vma=False,
    )
```

```python
import functools

import jax
import jax.numpy as jnp
from jax import lax
from jax.experimental import pallas as pl
from jax.experimental.pallas import tpu as pltpu
from jax.sharding import PartitionSpec as P

MESH = pl.DeviceIdType.MESH
NT = (((1,), (1,)), ((), ()))
F32 = jnp.float32
BF16 = jnp.bfloat16
LANES = 128


def dot_nt(left, right):
    return lax.dot_general(left, right, NT, preferred_element_type=F32)


def iota(shape, dim):
    return lax.broadcasted_iota(jnp.int32, shape, dim)


def hot(mask):
    return jnp.where(mask, 1.0, 0.0).astype(BF16)


def half_norm(x):
    return 0.5 * jnp.sum(jnp.square(x.astype(F32)), axis=1, keepdims=True)


def half_norm_row(x):
    square = jnp.square(x.astype(F32))
    folded = square[:, :LANES]
    for begin in range(LANES, square.shape[1], LANES):
        folded = folded + square[:, begin:begin + LANES]
    return 0.5 * jnp.sum(folded.T, axis=0, keepdims=True)


def each(n, fn):
    def step(k, carry):
        fn(k)
        return carry
    lax.fori_loop(0, n, step, 0)


def kernel(
    n_pts, n_ctr, panels, chunk, sub,
    pts_hbm, cls_hbm, tgt_hbm, cw_hbm, inv_hbm, idx_hbm, cen_hbm, coef_hbm, fac_hbm, pinv_hbm,
    grad_ref, sol_ref,
    pts, cls, tgt, cw, inv_row, idx, head,
    cen, coef, pinv_raw, pinv, fac_raw, fac, rnorm, pnorm, pall, kmat, ksel,
    sel, total_acc, part, part_recv, wt_send, wt_recv, rsend, rbuf,
    wsend, wrecv, wcount, wpack, wblk, solsend, solrecv, rhssend, rhsrecv, acc,
    loc, cen_sem, pt_sem, fw_sem, pr_sem, wt_sem, rs_sem, w_sem, so_s, so_r, rh_s, rh_r,
):
    p_me, c_me = lax.axis_index("pts"), lax.axis_index("ctr")
    rows, feats = pts.shape
    group = rows * n_ctr
    centers = cen.shape[0]
    targets = tgt.shape[1]
    tcols = targets // n_pts
    own_rows, panel_rows = pinv.shape
    owners = panel_rows // own_rows
    my_panel = c_me // owners
    chunks = centers // chunk
    blocks = rbuf.shape[0]
    pt_blocks = blocks // n_pts
    per_block = n_ctr // pt_blocks
    copies = n_ctr // blocks
    width = rows * per_block
    me = p_me * n_ctr + c_me
    blk = lax.rem(c_me, blocks)
    rep = c_me // blocks
    blk_pts = lax.rem(blk, n_pts)
    own_block = blk_pts == p_me

    def remote(src, dst, send, recv, p, c):
        return pltpu.make_async_remote_copy(
            src_ref=src, dst_ref=dst, send_sem=send, recv_sem=recv,
            device_id={"pts": p, "ctr": c}, device_id_type=MESH,
        )

    def arrived(ref, sem):
        remote(ref, ref, sem.at[0], sem.at[1], p_me, lax.rem(c_me + 1, n_ctr)).wait_recv()

    def departed(ref, sem):
        remote(ref, ref, sem.at[0], sem.at[1], p_me, lax.rem(c_me + 1, n_ctr)).wait_send()

    def unless(flag, most, fn):
        @pl.when(flag)
        def _():
            fn(most - 1)

        @pl.when(jnp.logical_not(flag))
        def _():
            fn(most)

    def local(src, dst, k):
        return pltpu.make_async_copy(src, dst, loc.at[k])

    def cen_copy(k):
        at = pl.ds(pl.multiple_of(k * chunk, chunk), chunk)
        return pltpu.make_async_copy(cen_hbm.at[at], cen.at[at], cen_sem.at[k])

    pts_copy = local(pts_hbm, pts, 0)
    inv_copy = local(inv_hbm, inv_row, 1)
    cls_copy = local(cls_hbm, cls, 2)
    cw_copy = local(cw_hbm, cw, 3)
    tgt_copy = local(tgt_hbm, tgt, 4)
    idx_copy = local(idx_hbm, idx, 5)
    head_copy = local(idx_hbm.at[pl.ds(0, head.shape[0])], head, 6)
    coef_copy = local(coef_hbm, coef, 7)
    pinv_copy = local(pinv_hbm, pinv_raw, 8)
    fac_copy = local(fac_hbm.at[:, pl.ds(0, fac.shape[1])], fac_raw, 9)
    pts_copy.start()
    inv_copy.start()

    barrier = pltpu.get_barrier_semaphore()

    def peer(k):
        if n_ctr & (n_ctr - 1):
            return lax.rem(c_me + k + 1, n_ctr)
        return lax.bitwise_xor(c_me, jnp.where(k == 0, 1, n_ctr - k))
    pair = p_me // 2 * 2

    def mate(k):
        return 2 * pair + 1 - p_me if k == 0 else lax.rem(pair + k + 1, n_pts)

    def source(k):
        p = lax.rem(p_me + k, n_pts)
        b = lax.rem(blk // n_pts + k // n_pts, pt_blocks)
        return p, b, rep * blocks + b * n_pts + p_me

    def greet(p, c):
        pl.semaphore_signal(barrier, inc=1, device_id={"pts": p, "ctr": c}, device_id_type=MESH)

    def foreign(k):
        return jnp.logical_or(k != 0, jnp.logical_not(own_block))

    each(n_ctr - 1, lambda k: greet(p_me, peer(k)))
    for k in range(n_pts - 1):
        greet(mate(k), c_me)

    def greet_source(k):
        @pl.when(foreign(k))
        def _():
            p, _, c = source(k)
            greet(p, c)
    each(blocks, greet_source)
    cls_copy.start()
    cw_copy.start()
    each(chunks, lambda k: cen_copy(k).start())
    idx_copy.start()
    tgt_copy.start()
    head_copy.start()
    coef_copy.start()

    pts_copy.wait()
    inv_copy.wait()
    inv = inv_row[...]
    own_slot = pl.ds(pl.multiple_of(me * rows, rows), rows)
    pall[own_slot, :] = (pts[...].astype(F32) * inv).astype(BF16)
    pl.semaphore_wait(barrier, n_ctr + n_pts - 2 + blocks - own_block.astype(jnp.int32))

    def pt_copy(c_src, c_dst):
        slot = pl.ds(pl.multiple_of((p_me * n_ctr + c_src) * rows, rows), rows)
        return remote(pall.at[slot], pall.at[slot], pt_sem.at[0], pt_sem.at[1], p_me, c_dst)
    each(n_ctr - 1, lambda k: pt_copy(c_me, peer(k)).start())

    cls_copy.wait()
    cw_copy.wait()
    lane_of = lax.rem(c_me, per_block) * rows
    place = hot(iota((rows, width), 1) == iota((rows, width), 0) + lane_of)
    label = jnp.dot(
        jnp.broadcast_to(cls[...].astype(F32).astype(BF16), (8, rows)), place, preferred_element_type=F32
    )
    mine_lane = (iota((8, width), 1) >= lane_of) & (iota((8, width), 1) < lane_of + rows)
    weight = jnp.zeros((8, width), F32)
    for k in range(cw.shape[1]):
        weight = jnp.where(mine_lane & (label == float(k)), cw[0, k], weight)
    wt_send[...] = weight

    def wt_dest(k):
        turn = lax.rem(c_me + k, per_block)
        return turn // n_pts * blocks + c_me // per_block * n_pts + lax.rem(turn, n_pts)

    def wt_copy(c_src, c_dst):
        at = lax.rem(c_src, per_block)
        return remote(wt_send, wt_recv.at[at], wt_sem.at[0], wt_sem.at[1], p_me, c_dst)

    def not_me(c, fn):
        @pl.when(c != c_me)
        def _():
            fn(c)
    each(per_block, lambda k: not_me(wt_dest(k), lambda c: wt_copy(c_me, c).start()))

    own_weights = c_me // per_block == blk // n_pts

    @pl.when(own_weights)
    def _():
        wt_recv[lax.rem(c_me, per_block)] = weight

    step = 256

    def scale(k):
        at = pl.ds(pl.multiple_of(k * step, step), step)
        scaled = (cen[at, :].astype(F32) * inv).astype(BF16)
        cen[at, :] = scaled
        rnorm[0:1, at] = half_norm_row(scaled)

    def scale_chunk(k):
        cen_copy(k).wait()
        each(chunk // step, lambda j: scale(k * (chunk // step) + j))
    each(chunks, scale_chunk)

    idx_copy.wait()
    shift, wide_lanes = 64, idx.shape[1]
    per = wide_lanes // n_ctr
    slots = sel.shape[0]
    relative = idx[...] - c_me * centers
    relative = jnp.where((relative >= 0) & (relative < centers), relative, 0)
    fold = hot(iota((wide_lanes, wide_lanes), 0) // n_ctr == iota((wide_lanes, wide_lanes), 1))
    spread = hot(iota((slots, relative.shape[0]), 0) // per == iota((slots, relative.shape[0]), 1))

    def column(value):
        folded = jnp.dot(value.astype(F32).astype(BF16), fold, preferred_element_type=F32)
        return jnp.dot(spread, folded.astype(BF16), preferred_element_type=F32)
    both = shift * column(relative // shift) + column(lax.rem(relative, shift))
    at_lane = lax.rem(iota((slots, wide_lanes), 0), per) == iota((slots, wide_lanes), 1)
    local_row = jnp.sum(jnp.where(at_lane, both, 0.0), axis=1, keepdims=True).astype(jnp.int32)
    coef_copy.wait()
    tgt_copy.wait()
    head_copy.wait()
    pinv_copy.start()
    fac_copy.start()

    arrived(pall.at[pl.ds(0, (n_ctr - 1) * rows)], pt_sem)

    def group_at(p):
        return pl.ds(pl.multiple_of(p * group, group), group)

    def fw_copy(p_src, p_dst):
        at = group_at(p_src)
        return remote(pall.at[at], pall.at[at], fw_sem.at[0], fw_sem.at[1], p_dst, c_me)
    for k in range(n_pts - 1):
        fw_copy(p_me, mate(k)).start()

    def sub_at(k, j):
        return pl.ds(pl.multiple_of(k * chunk + j * sub, sub), sub)

    def kernel_block(left, norm, at):
        return jnp.exp(dot_nt(left, cen[at, :]) - norm - rnorm[0:1, at]).astype(BF16)
    mine = pall[group_at(p_me), :]
    mine_norm = half_norm(mine)
    pnorm[group_at(p_me), :] = jnp.broadcast_to(mine_norm, (group, LANES))
    total = jnp.zeros((group, targets), F32)
    for k in range(chunks):
        at = pl.ds(k * chunk, chunk)
        block = kernel_block(mine, mine_norm, at)
        kmat[group_at(p_me), at] = block
        total = total + jnp.dot(block, coef[at, :], preferred_element_type=F32)
    total_acc[...] = total
    own_rows_at = pl.ds(pl.multiple_of(c_me * rows, rows), rows)
    total_acc[own_rows_at, :] = total_acc[own_rows_at, :] - tgt[...]
    for b in range(pt_blocks):
        turned = total_acc[b * width:(b + 1) * width, :].T
        for q in range(n_pts):
            part[b * n_pts + q] = turned[q * tcols:(q + 1) * tcols]

    def pr_copy(c_src, c_dst):
        return remote(
            part.at[lax.rem(c_dst, blocks)], part_recv.at[c_src], pr_sem.at[0], pr_sem.at[1], p_me, c_dst
        )
    each(n_ctr - 1, lambda k: pr_copy(c_me, peer(k)).start())
    part_recv[c_me] = part[blk]

    sel[...] = jnp.zeros_like(sel)

    def select(k):
        at = pl.ds(pl.multiple_of(k * chunk, chunk), chunk)
        picked = hot(iota((slots, chunk), 1) == local_row - k * chunk)
        sel[...] += jnp.dot(picked, cen[at, :], preferred_element_type=F32)
    each(chunks, select)

    unless(own_weights, per_block, lambda n: arrived(wt_recv.at[pl.ds(0, n)], wt_sem))
    weights = jnp.sum(wt_recv[...], axis=0)[0:1]
    arrived(part_recv.at[pl.ds(0, n_ctr - 1)], pr_sem)
    residual = (weights * jnp.sum(part_recv[...], axis=0)).astype(BF16)
    rsend[...] = residual

    def rs_slot(p, b):
        return p * pt_blocks + b

    def rs_copy(p_src, b_src, p_dst, c_dst):
        at = rs_slot(p_src, b_src)
        return remote(rsend, rbuf.at[at], rs_sem.at[0], rs_sem.at[1], p_dst, c_dst)

    def rs_out(k):
        return rs_copy(p_me, blk // n_pts, blk_pts, rep * blocks + lax.rem(blk + k, blocks))

    def rs_start(k):
        @pl.when(foreign(k))
        def _():
            rs_out(k).start()
    each(blocks, rs_start)

    @pl.when(own_block)
    def _():
        rbuf[rs_slot(p_me, blk // n_pts)] = residual

    arrived(pall.at[pl.ds(0, (n_pts - 1) * group)], fw_sem)
    together = n_pts - 1 if group * n_pts <= 512 else 1
    for first in range(0, n_pts - 1, together):
        mates = [mate(k) for k in range(first, first + together)]
        left = jnp.concatenate([pall[group_at(p), :] for p in mates], axis=0)
        left_norm = half_norm(left)
        for k, p in enumerate(mates):
            pnorm[group_at(p), :] = jnp.broadcast_to(left_norm[k * group:(k + 1) * group], (group, LANES))

        def fill(k):
            for j in range(chunk // sub):
                at = sub_at(k, j)
                block = kernel_block(left, left_norm, at)
                for n, p in enumerate(mates):
                    kmat[group_at(p), at] = block[n * group:(n + 1) * group]
        each(chunks, fill)

    chosen = sel[...].astype(BF16)
    chosen_norm = half_norm(chosen)
    span = 512

    def window_kernel(k):
        at = pl.ds(pl.multiple_of(k * span, span), span)
        norm = pnorm[at, :].T[0:1]
        ksel[:, at] = jnp.exp(dot_nt(chosen, pall[at, :]) - norm - chosen_norm).astype(BF16)
    each(pall.shape[0] // span, window_kernel)

    unless(own_block, blocks, lambda n: arrived(rbuf.at[pl.ds(0, n)], rs_sem))

    wide_t = jnp.concatenate([rbuf[b] for b in range(blocks)], axis=1)
    tall_t = jnp.concatenate([wide_t] * n_pts, axis=0)
    pieces, run = wsend.shape[1], wsend.shape[2]
    fine = pieces > 1
    lane_group = iota((run, targets), 1) // tcols
    per_panel = slots // panels

    def pack(panel):
        window = dot_nt(ksel[panel * per_panel:(panel + 1) * per_panel], tall_t)
        for g in range(pieces):
            packed = jnp.zeros((run, targets), F32)
            for h in range(n_pts):
                begin = (g * n_pts + h) * run
                packed = packed + jnp.where(lane_group == h, window[begin:begin + run], 0.0)
            wsend[panel, g] = packed.astype(BF16)
    own_piece = lax.rem(c_me, owners) * pieces // owners

    def w_first(d, c_dst):
        return remote(
            wsend.at[0, pl.ds(0, d + 1)], wrecv.at[c_me, pl.ds(0, d + 1)], w_sem.at[0], w_sem.at[1], p_me, c_dst
        )

    def w_later(c_dst):
        d = lax.rem(c_dst, owners) * pieces // owners
        return remote(
            wsend.at[c_dst // owners, pl.ds(d, 1)], wrecv.at[c_me, pl.ds(d, 1)], w_sem.at[0], w_sem.at[1], p_me, c_dst
        )
    alike = owners // pieces
    pack(0)
    for d in range(pieces):
        each(alike, lambda j: not_me(d * alike + j, lambda c: w_first(d, c).start()))
    for panel in range(1, panels):
        pack(panel)
    each((panels - 1) * owners, lambda j: not_me(owners + j, lambda c: w_later(c).start()))
    wrecv[c_me] = wsend[my_panel]

    def backward(k):
        at = pl.ds(pl.multiple_of(k * chunk, chunk), chunk)
        grad_ref[:, at] = jnp.dot(wide_t, kmat[:, at], preferred_element_type=F32)
    each(chunks, backward)
    pinv_copy.wait()
    fac_copy.wait()
    pinv[...] = pinv_raw[...].astype(BF16)

    departed(pall.at[pl.ds(0, (n_ctr - 1) * rows)], pt_sem)
    unless(own_weights, per_block, lambda n: departed(wt_recv.at[pl.ds(0, n)], wt_sem))
    departed(pall.at[pl.ds(0, (n_pts - 1) * group)], fw_sem)
    departed(part_recv.at[pl.ds(0, n_ctr - 1)], pr_sem)
    unless(own_block, blocks, lambda n: departed(rbuf.at[pl.ds(0, n)], rs_sem))

    w_total = sum((d + 1) * alike for d in range(pieces)) + (panels - 1) * owners

    def w_departed(own):
        departed(wcount.at[pl.ds(0, w_total - own)], w_sem)

    def unpack(g):
        for o in range(n_ctr):
            shard = head[o // wide_lanes, o % wide_lanes] // centers
            wpack[g, pl.ds(o, run, stride=n_ctr), :] = wrecv[shard, g].astype(F32)

    halves = solsend.shape[0]

    def so_copy(c_src, c_dst, h):
        at = c_src * halves + h
        return remote(solsend.at[h], solrecv.at[at], so_s.at[0], so_r.at[at], p_me, c_dst)

    def rh_copy(c_src, c_dst):
        at = lax.rem(c_src, owners)
        return remote(rhssend, rhsrecv.at[at], rh_s.at[lax.rem(c_dst, owners)], rh_r.at[at], p_me, c_dst)

    half_rows = own_rows // halves

    def send_solved(panel, h, result):
        sol_ref[:, h * half_rows:(h + 1) * half_rows] = result
        solsend[h] = result.astype(BF16)
        later = (panels - 1 - panel) * owners
        each(later, lambda k: so_copy(c_me, (panel + 1) * owners + k, h).start())

    def departed_so(n):
        ref = solrecv.at[pl.ds(0, n * halves)]
        remote(ref, ref, so_s.at[0], so_r.at[0], p_me, lax.rem(c_me + 1, n_ctr)).wait_send()

    def first_panel(d):
        arrived(wrecv.at[pl.ds(0, n_ctr - 1), pl.ds(0, d + 1)], w_sem)
        span_rows = panel_rows // (pieces * n_pts)
        parts = []
        for g in range(d + 1):
            unpack(g)
        for g in range(d + 1):
            turned = wpack[g].T.astype(BF16)
            parts += [turned[h * tcols:(h + 1) * tcols] for h in range(n_pts)]
        rhs = jnp.concatenate(parts, axis=1)
        for h in range(halves):
            rows_at = slice(h * half_rows, (h + 1) * half_rows)
            send_solved(0, h, dot_nt(rhs, pinv[rows_at, :(d + 1) * n_pts * span_rows]))
        if panels > 1:
            departed_so((panels - 1) * owners)
        w_departed(d + 1)

    for d in range(pieces):
        @pl.when((my_panel == 0) & (own_piece == d))
        def _():
            first_panel(d)

    for panel in range(1, panels):
        @pl.when(my_panel == panel)
        def _():
            done = panel * owners
            position = c_me - done
            arrived(wrecv.at[pl.ds(0, n_ctr - 1), pl.ds(0, 1)], w_sem)
            fac[...] = fac_raw[...].astype(BF16)
            unpack(own_piece)
            if fine:
                turned = wpack[own_piece].T
                own = jnp.concatenate([turned[h * tcols:(h + 1) * tcols] for h in range(n_pts)], axis=1)
            else:
                offset = position * own_rows
                part_len = panel_rows // n_pts
                within = pl.multiple_of(lax.rem(offset, part_len), own_rows)
                turned = wpack[0, pl.ds(within, own_rows), :].T
                for g in range(n_pts):
                    wblk[g] = turned[g * tcols:(g + 1) * tcols]
                own = wblk[offset // part_len]
            if fine:
                for b in range(done):
                    for h in range(halves):
                        so_copy(b, b, h).wait_recv()
                        begin = b * own_rows + h * half_rows
                        own = own - dot_nt(solrecv[b * halves + h], fac[:, begin:begin + half_rows])
            else:
                each(done, lambda k: so_copy(k, k, 0).wait_recv())
                solved = jnp.concatenate([solrecv[b] for b in range(done)], axis=1)
                own = own - dot_nt(solved, fac[:, :done * own_rows])
            rhssend[...] = own.astype(BF16)

            def below(k, fn):
                @pl.when(k > position if fine else k != position)
                def _():
                    fn(done + k)
            each(owners, lambda k: below(owners - 1 - k, lambda c: rh_copy(c_me, c).start()))
            if fine:
                acc[...] = jnp.zeros_like(acc)
                rhsrecv[position] = rhssend[...]
                for b in range(owners):
                    @pl.when(b <= position)
                    def _():
                        @pl.when(b < position)
                        def _():
                            rh_copy(done + b, done + b).wait_recv()
                        acc[...] += dot_nt(rhsrecv[b], pinv[:, b * own_rows:(b + 1) * own_rows])
                result = acc[...]
            else:
                rhsrecv[position] = rhssend[...]
                each(owners, lambda k: below(k, lambda c: rh_copy(c, c).wait_recv()))
                result = dot_nt(jnp.concatenate([rhsrecv[b] for b in range(owners)], axis=1), pinv[...])
            later = (panels - 1 - panel) * owners
            if later:
                for h in range(halves):
                    send_solved(panel, h, result[:, h * half_rows:(h + 1) * half_rows])
                departed_so(later)
            else:
                sol_ref[...] = result
            each(owners, lambda k: below(k, lambda c: rh_copy(c_me, c).wait_send()))
            w_departed(1)


def emit(grad_ref, sol_ref, grad_out, sol_out, sem):
    first = pltpu.make_async_copy(grad_ref, grad_out, sem.at[0])
    second = pltpu.make_async_copy(sol_ref, sol_out, sem.at[1])
    first.start()
    second.start()
    first.wait()
    second.wait()


def body(
    points, point_class, targets, class_weight, inv_scale, centers, coefficients, center_index, factor, panel_inverse
):
    n_pts, n_ctr = lax.axis_size("pts"), lax.axis_size("ctr")
    rows, feats = points.shape
    n_cen, n_tgt = coefficients.shape
    tcols = n_tgt // n_pts
    own_rows, panel_rows = panel_inverse.shape
    panels = factor.shape[1] // panel_rows
    owners = panel_rows // own_rows
    total = rows * n_pts * n_ctr
    group = rows * n_ctr
    per_block = LANES // rows
    pt_blocks = n_ctr // per_block
    blocks = n_pts * pt_blocks
    slots = center_index.shape[0] // n_ctr
    pieces = owners if own_rows % LANES == 0 else 1
    halves = 1
    run = slots // panels // pieces // n_pts
    w_most = pieces * (pieces + 1) // 2 * (owners // pieces) + (panels - 1) * owners
    solved_cols = panel_rows * (panels - 1)
    chunk = 1024
    index = center_index.reshape(-1, LANES)
    vmem = pl.BlockSpec(memory_space=pltpu.VMEM)
    hbm = pl.BlockSpec(memory_space=pltpu.HBM)
    dma = pltpu.SemaphoreType.DMA
    scratch = [
        pltpu.VMEM((rows, feats), BF16),
        pltpu.VMEM((1, rows), jnp.int32),
        pltpu.VMEM((rows, n_tgt), F32),
        pltpu.SMEM((1, class_weight.shape[0]), F32),
        pltpu.VMEM((1, feats), F32),
        pltpu.VMEM(index.shape, jnp.int32),
        pltpu.SMEM((8, LANES), jnp.int32),
        pltpu.VMEM((n_cen, feats), BF16),
        pltpu.VMEM((n_cen, n_tgt), BF16),
        pltpu.VMEM((own_rows, panel_rows), F32),
        pltpu.VMEM((own_rows, panel_rows), BF16),
        pltpu.VMEM((own_rows, solved_cols), F32),
        pltpu.VMEM((own_rows, solved_cols), BF16),
        pltpu.VMEM((8, n_cen), F32),
        pltpu.VMEM((total, LANES), F32),
        pltpu.VMEM((total, feats), BF16),
        pltpu.VMEM((total, n_cen), BF16),
        pltpu.VMEM((slots, total), BF16),
        pltpu.VMEM((slots, feats), F32),
        pltpu.VMEM((group, n_tgt), F32),
        pltpu.VMEM((blocks, tcols, LANES), F32),
        pltpu.VMEM((n_ctr, tcols, LANES), F32),
        pltpu.VMEM((8, LANES), F32),
        pltpu.VMEM((per_block, 8, LANES), F32),
        pltpu.VMEM((tcols, LANES), BF16),
        pltpu.VMEM((blocks, tcols, LANES), BF16),
        pltpu.VMEM((panels, pieces, run, n_tgt), BF16),
        pltpu.VMEM((n_ctr, pieces, run, n_tgt), BF16),
        pltpu.VMEM((w_most, run, n_tgt), BF16),
        pltpu.VMEM((pieces, run * n_ctr, n_tgt), F32),
        pltpu.VMEM((n_pts, tcols, own_rows), F32),
        pltpu.VMEM((halves, tcols, own_rows // halves), BF16),
        pltpu.VMEM((owners * (panels - 1) * halves, tcols, own_rows // halves), BF16),
        pltpu.VMEM((tcols, own_rows), BF16),
        pltpu.VMEM((owners, tcols, own_rows), BF16),
        pltpu.VMEM((tcols, own_rows), F32),
        dma((10,)), dma((n_cen // chunk,)),
        dma((2,)), dma((2,)), dma((2,)), dma((2,)), dma((2,)), dma((2,)),
        dma((1,)), dma((owners * (panels - 1) * halves,)),
        dma((owners,)), dma((owners,)),
    ]
    grad, solved = pl.pallas_call(
        functools.partial(kernel, n_pts, n_ctr, panels, chunk, 256),
        out_shape=(
            pltpu.VMEM((tcols, n_cen), F32),
            pltpu.VMEM((tcols, own_rows), F32),
        ),
        in_specs=[hbm] * 10,
        out_specs=(vmem, vmem),
        scratch_shapes=scratch,
        compiler_params=pltpu.CompilerParams(
            collective_id=0, has_side_effects=True, vmem_limit_bytes=60000000
        ),
        name="falkon",
    )(
        points, point_class[None, :], targets, class_weight[None, :], inv_scale[None, :],
        index, centers, coefficients, factor, panel_inverse,
    )
    grad, solved = pl.pallas_call(
        emit,
        out_shape=(
            jax.ShapeDtypeStruct((tcols, n_cen), F32),
            jax.ShapeDtypeStruct((tcols, own_rows), F32),
        ),
        in_specs=[vmem, vmem],
        out_specs=(hbm, hbm),
        scratch_shapes=[dma((2,))],
        compiler_params=pltpu.CompilerParams(vmem_limit_bytes=1048576),
        name="emit",
    )(grad, solved)
    return grad.T, solved.T


def solution(mesh):
    placed = (
        P(("pts", "ctr"), None),
        P(("pts", "ctr")),
        P(("pts", "ctr"), None),
        P(),
        P(),
        P("ctr", None),
        P("ctr", None),
        P(),
        P("ctr", None),
        P("ctr", None),
    )
    return jax.shard_map(
        body,
        mesh=mesh,
        in_specs=placed,
        out_specs=(P("ctr", "pts"), P("ctr", "pts")),
        check_vma=False,
    )
```

```python
import functools

import jax
import jax.numpy as jnp
from jax import lax
from jax.experimental import pallas as pl
from jax.experimental.pallas import tpu as pltpu
from jax.sharding import PartitionSpec as P

MESH = pl.DeviceIdType.MESH
NT = (((1,), (1,)), ((), ()))
F32 = jnp.float32
BF16 = jnp.bfloat16
LANES = 128


def dot_nt(left, right):
    return lax.dot_general(left, right, NT, preferred_element_type=F32)


def iota(shape, dim):
    return lax.broadcasted_iota(jnp.int32, shape, dim)


def hot(mask):
    return jnp.where(mask, 1.0, 0.0).astype(BF16)


def half_norm(x):
    return 0.5 * jnp.sum(jnp.square(x.astype(F32)), axis=1, keepdims=True)


def half_norm_row(x):
    square = jnp.square(x.astype(F32))
    folded = square[:, :LANES]
    for begin in range(LANES, square.shape[1], LANES):
        folded = folded + square[:, begin:begin + LANES]
    return 0.5 * jnp.sum(folded.T, axis=0, keepdims=True)


def each(n, fn):
    def step(k, carry):
        fn(k)
        return carry
    lax.fori_loop(0, n, step, 0)


def unrolled(n, fn):
    if n > 8:
        return each(n, fn)
    for k in range(n):
        fn(k)


def kernel(
    n_pts, n_ctr, panels, chunk, sub,
    pts_hbm, cls_hbm, tgt_hbm, cw_hbm, inv_hbm, idx_hbm, cen_hbm, coef_hbm, fac_hbm, pinv_hbm,
    grad_ref, sol_ref,
    pts, cls, tgt, cw, inv_row, idx, head,
    cen, coef, pinv_raw, pinv, fac_raw, fac, rnorm, pnorm, pall, kmat, ksel,
    sel, total_acc, part, part_recv, wt_send, wt_recv, rsend, rbuf, rcount,
    wsend, wrecv, wcount, wpack, wblk, solsend, solrecv, rhssend, rhsrecv, acc,
    loc, cen_sem, pt_sem, fw_sem, pr_sem, wt_sem, rs_sem, w_sem, so_s, so_r, rh_s, rh_r,
):
    p_me, c_me = lax.axis_index("pts"), lax.axis_index("ctr")
    rows, feats = pts.shape
    group = rows * n_ctr
    centers = cen.shape[0]
    targets = tgt.shape[1]
    tcols = targets // n_pts
    own_rows, panel_rows = pinv.shape
    owners = panel_rows // own_rows
    my_panel = c_me // owners
    chunks = centers // chunk
    blocks = rbuf.shape[0]
    pt_blocks = blocks // n_pts
    per_block = n_ctr // pt_blocks
    width = rows * per_block
    me = p_me * n_ctr + c_me
    first_red = (n_ctr - blocks) // 2
    reduces = (c_me >= first_red) & (c_me < first_red + blocks)
    blk = jnp.where(reduces, c_me - first_red, 0)
    blk_pts = lax.rem(blk + p_me // 2 * 2, n_pts)
    own_block = reduces & (blk_pts == p_me)

    def remote(src, dst, send, recv, p, c):
        return pltpu.make_async_remote_copy(
            src_ref=src, dst_ref=dst, send_sem=send, recv_sem=recv,
            device_id={"pts": p, "ctr": c}, device_id_type=MESH,
        )

    def arrived(ref, sem):
        remote(ref, ref, sem.at[0], sem.at[1], p_me, lax.rem(c_me + 1, n_ctr)).wait_recv()

    def departed(ref, sem):
        remote(ref, ref, sem.at[0], sem.at[1], p_me, lax.rem(c_me + 1, n_ctr)).wait_send()

    def unless(flag, most, fn):
        @pl.when(flag)
        def _():
            fn(most - 1)

        @pl.when(jnp.logical_not(flag))
        def _():
            fn(most)

    def local(src, dst, k):
        return pltpu.make_async_copy(src, dst, loc.at[k])

    def cen_copy(k):
        at = pl.ds(pl.multiple_of(k * chunk, chunk), chunk)
        return pltpu.make_async_copy(cen_hbm.at[at], cen.at[at], cen_sem.at[k])

    pts_copy = local(pts_hbm, pts, 0)
    inv_copy = local(inv_hbm, inv_row, 1)
    cls_copy = local(cls_hbm, cls, 2)
    cw_copy = local(cw_hbm, cw, 3)
    tgt_copy = local(tgt_hbm, tgt, 4)
    idx_copy = local(idx_hbm, idx, 5)
    head_copy = local(idx_hbm.at[pl.ds(0, head.shape[0])], head, 6)
    coef_copy = local(coef_hbm, coef, 7)
    pinv_copy = local(pinv_hbm, pinv_raw, 8)
    fac_copy = local(fac_hbm.at[:, pl.ds(0, fac.shape[1])], fac_raw, 9)
    pts_copy.start()
    inv_copy.start()

    barrier = pltpu.get_barrier_semaphore()

    def peer(k):
        above = n_ctr - 1 - c_me
        low = jnp.where(k < above, n_ctr - 1 - k, k - above)
        high = jnp.where(k < c_me, k, n_ctr - 1 - k + c_me)
        return jnp.where(c_me < above, low, high)
    pair = p_me // 2 * 2

    def mate(k):
        return 2 * pair + 1 - p_me if k == 0 else lax.rem(pair + k + 1, n_pts)

    def greet(p, c):
        pl.semaphore_signal(barrier, inc=1, device_id={"pts": p, "ctr": c}, device_id_type=MESH)

    each(n_ctr - 1, lambda k: greet(p_me, peer(k)))
    for k in range(n_pts - 1):
        greet(mate(k), c_me)

    cls_copy.start()
    cw_copy.start()
    each(chunks, lambda k: cen_copy(k).start())
    idx_copy.start()
    tgt_copy.start()
    head_copy.start()
    coef_copy.start()

    pts_copy.wait()
    inv_copy.wait()
    inv = inv_row[...]
    own_slot = pl.ds(pl.multiple_of(me * rows, rows), rows)
    pall[own_slot, :] = (pts[...].astype(F32) * inv).astype(BF16)
    pl.semaphore_wait(barrier, n_ctr + n_pts - 2)

    def pt_copy(c_src, c_dst):
        slot = pl.ds(pl.multiple_of((p_me * n_ctr + c_src) * rows, rows), rows)
        return remote(pall.at[slot], pall.at[slot], pt_sem.at[0], pt_sem.at[1], p_me, c_dst)
    each(n_ctr - 1, lambda k: pt_copy(c_me, peer(k)).start())

    cls_copy.wait()
    cw_copy.wait()
    lane_of = lax.rem(c_me, per_block) * rows
    place = hot(iota((rows, width), 1) == iota((rows, width), 0) + lane_of)
    label = jnp.dot(
        jnp.broadcast_to(cls[...].astype(F32).astype(BF16), (8, rows)), place, preferred_element_type=F32
    )
    mine_lane = (iota((8, width), 1) >= lane_of) & (iota((8, width), 1) < lane_of + rows)
    weight = jnp.zeros((8, width), F32)
    for k in range(cw.shape[1]):
        weight = jnp.where(mine_lane & (label == float(k)), cw[0, k], weight)
    wt_send[...] = weight

    def wt_dest(k):
        return first_red + c_me // per_block * n_pts + k

    def wt_copy(c_src, c_dst):
        at = lax.rem(c_src, per_block)
        return remote(wt_send, wt_recv.at[at], wt_sem.at[0], wt_sem.at[1], p_me, c_dst)

    def not_me(c, fn):
        @pl.when(c != c_me)
        def _():
            fn(c)
    each(n_pts, lambda k: not_me(wt_dest(k), lambda c: wt_copy(c_me, c).start()))

    own_weights = reduces & (c_me // per_block == blk // n_pts)

    @pl.when(own_weights)
    def _():
        wt_recv[lax.rem(c_me, per_block)] = weight

    step = 256

    def scale(k):
        at = pl.ds(pl.multiple_of(k * step, step), step)
        scaled = (cen[at, :].astype(F32) * inv).astype(BF16)
        cen[at, :] = scaled
        rnorm[0:1, at] = half_norm_row(scaled)

    def scale_chunk(k):
        cen_copy(k).wait()
        unrolled(chunk // step, lambda j: scale(k * (chunk // step) + j))
    each(chunks, scale_chunk)

    idx_copy.wait()
    shift, wide_lanes = 64, idx.shape[1]
    per = wide_lanes // n_ctr
    slots = sel.shape[0]
    relative = idx[...] - c_me * centers
    relative = jnp.where((relative >= 0) & (relative < centers), relative, 0)
    fold = hot(iota((wide_lanes, wide_lanes), 0) // n_ctr == iota((wide_lanes, wide_lanes), 1))
    spread = hot(iota((slots, relative.shape[0]), 0) // per == iota((slots, relative.shape[0]), 1))

    def column(value):
        folded = jnp.dot(value.astype(F32).astype(BF16), fold, preferred_element_type=F32)
        return jnp.dot(spread, folded.astype(BF16), preferred_element_type=F32)
    both = shift * column(relative // shift) + column(lax.rem(relative, shift))
    at_lane = lax.rem(iota((slots, wide_lanes), 0), per) == iota((slots, wide_lanes), 1)
    local_row = jnp.sum(jnp.where(at_lane, both, 0.0), axis=1, keepdims=True).astype(jnp.int32)
    coef_copy.wait()
    tgt_copy.wait()
    head_copy.wait()
    pinv_copy.start()
    fac_copy.start()

    arrived(pall.at[pl.ds(0, (n_ctr - 1) * rows)], pt_sem)

    def group_at(p):
        return pl.ds(pl.multiple_of(p * group, group), group)

    def fw_copy(p_src, p_dst):
        at = group_at(p_src)
        return remote(pall.at[at], pall.at[at], fw_sem.at[0], fw_sem.at[1], p_dst, c_me)
    for k in range(n_pts - 1):
        fw_copy(p_me, mate(k)).start()

    def sub_at(k, j):
        return pl.ds(pl.multiple_of(k * chunk + j * sub, sub), sub)

    def kernel_block(left, norm, at):
        return jnp.exp(dot_nt(left, cen[at, :]) - norm - rnorm[0:1, at]).astype(BF16)
    mine = pall[group_at(p_me), :]
    mine_norm = half_norm(mine)
    pnorm[group_at(p_me), :] = jnp.broadcast_to(mine_norm, (group, LANES))
    total = jnp.zeros((group, targets), F32)
    for k in range(chunks):
        at = pl.ds(k * chunk, chunk)
        block = kernel_block(mine, mine_norm, at)
        kmat[group_at(p_me), at] = block
        total = total + jnp.dot(block, coef[at, :], preferred_element_type=F32)
    total_acc[...] = total
    own_rows_at = pl.ds(pl.multiple_of(c_me * rows, rows), rows)
    total_acc[own_rows_at, :] = total_acc[own_rows_at, :] - tgt[...]
    for b in range(pt_blocks):
        turned = total_acc[b * width:(b + 1) * width, :].T
        for q in range(n_pts):
            part[b * n_pts + q] = turned[q * tcols:(q + 1) * tcols]

    def part_of(b):
        return b // n_pts * n_pts + lax.rem(b + p_me // 2 * 2, n_pts)

    def pr_copy(c_src, c_dst):
        return remote(
            part.at[part_of(c_dst - first_red)], part_recv.at[c_src], pr_sem.at[0], pr_sem.at[1], p_me, c_dst
        )
    def pr_dest(k):
        return jnp.where(c_me < n_ctr // 2, first_red + blocks - 1 - k, first_red + k)
    each(blocks, lambda k: not_me(pr_dest(k), lambda c: pr_copy(c_me, c).start()))
    part_recv[c_me] = part[part_of(blk)]

    sel[...] = jnp.zeros_like(sel)

    def select(k):
        at = pl.ds(pl.multiple_of(k * chunk, chunk), chunk)
        picked = hot(iota((slots, chunk), 1) == local_row - k * chunk)
        return jnp.dot(picked, cen[at, :], preferred_element_type=F32)
    sel[...] = functools.reduce(lambda a, k: a + select(k), range(1, chunks), select(0))

    arrived(pall.at[pl.ds(0, (n_pts - 1) * group)], fw_sem)

    def rs_slot(p, b):
        return p * pt_blocks + b

    def rs_copy(c_dst):
        at = rs_slot(p_me, blk // n_pts)
        return remote(rsend, rbuf.at[at], rs_sem.at[0], rs_sem.at[1], blk_pts, c_dst)

    @pl.when(reduces)
    def _():
        unless(own_weights, per_block, lambda n: arrived(wt_recv.at[pl.ds(0, n)], wt_sem))
        weights = jnp.sum(wt_recv[...], axis=0)[0:1]
        arrived(part_recv.at[pl.ds(0, n_ctr - 1)], pr_sem)
        residual = (weights * jnp.sum(part_recv[...], axis=0)).astype(BF16)
        rsend[...] = residual

        @pl.when(own_block)
        def _():
            rbuf[rs_slot(p_me, blk // n_pts)] = residual
            each(n_ctr - 1, lambda k: rs_copy(peer(k)).start())

        @pl.when(jnp.logical_not(own_block))
        def _():
            each(n_ctr - 1, lambda k: rs_copy(peer(k)).start())
            rs_copy(c_me).start()

    together = n_pts - 1 if group * n_pts <= 512 else 1
    for first in range(0, n_pts - 1, together):
        mates = [mate(k) for k in range(first, first + together)]
        left = jnp.concatenate([pall[group_at(p), :] for p in mates], axis=0)
        left_norm = half_norm(left)
        for k, p in enumerate(mates):
            pnorm[group_at(p), :] = jnp.broadcast_to(left_norm[k * group:(k + 1) * group], (group, LANES))

        def fill(k):
            for j in range(chunk // sub):
                at = sub_at(k, j)
                block = kernel_block(left, left_norm, at)
                for n, p in enumerate(mates):
                    kmat[group_at(p), at] = block[n * group:(n + 1) * group]
        unrolled(chunks, fill)

    chosen = sel[...].astype(BF16)
    chosen_norm = half_norm(chosen)
    span = 512

    def window_kernel(k):
        at = pl.ds(pl.multiple_of(k * span, span), span)
        norm = pnorm[at, :].T[0:1]
        ksel[:, at] = jnp.exp(dot_nt(chosen, pall[at, :]) - norm - chosen_norm).astype(BF16)
    each(pall.shape[0] // span, window_kernel)

    unless(own_block, blocks, lambda n: arrived(rbuf.at[pl.ds(0, n)], rs_sem))

    wide_t = jnp.concatenate([rbuf[b] for b in range(blocks)], axis=1)
    tall_t = jnp.concatenate([wide_t] * n_pts, axis=0)
    pieces, run = wsend.shape[1], wsend.shape[2]
    fine = pieces > 1
    lane_group = iota((run, targets), 1) // tcols
    per_panel = slots // panels

    def pack(panel):
        window = dot_nt(ksel[panel * per_panel:(panel + 1) * per_panel], tall_t)
        for g in range(pieces):
            packed = jnp.zeros((run, targets), F32)
            for h in range(n_pts):
                begin = (g * n_pts + h) * run
                packed = packed + jnp.where(lane_group == h, window[begin:begin + run], 0.0)
            wsend[panel, g] = packed.astype(BF16)
    own_piece = lax.rem(c_me, owners) * pieces // owners

    def w_first(d, c_dst):
        return remote(
            wsend.at[0, pl.ds(0, d + 1)], wrecv.at[c_me, pl.ds(0, d + 1)], w_sem.at[0], w_sem.at[1], p_me, c_dst
        )

    def w_later(c_dst):
        d = lax.rem(c_dst, owners) * pieces // owners
        return remote(
            wsend.at[c_dst // owners, pl.ds(d, 1)], wrecv.at[c_me, pl.ds(d, 1)], w_sem.at[0], w_sem.at[1], p_me, c_dst
        )
    alike = owners // pieces
    pack(0)
    for d in range(pieces):
        each(alike, lambda j: not_me(d * alike + j, lambda c: w_first(d, c).start()))
    for panel in range(1, panels):
        pack(panel)
    each((panels - 1) * owners, lambda j: not_me(owners + j, lambda c: w_later(c).start()))
    wrecv[c_me] = wsend[my_panel]

    def backward(k):
        at = pl.ds(pl.multiple_of(k * chunk, chunk), chunk)
        grad_ref[:, at] = jnp.dot(wide_t, kmat[:, at], preferred_element_type=F32)
    unrolled(chunks, backward)
    pinv_copy.wait()
    fac_copy.wait()
    pinv[...] = pinv_raw[...].astype(BF16)

    departed(pall.at[pl.ds(0, (n_ctr - 1) * rows)], pt_sem)
    unless(own_weights, n_pts, lambda n: departed(wt_recv.at[pl.ds(0, n)], wt_sem))
    departed(pall.at[pl.ds(0, (n_pts - 1) * group)], fw_sem)
    unless(reduces, blocks, lambda n: departed(part.at[pl.ds(0, n)], pr_sem))

    @pl.when(reduces)
    def _():
        unless(own_block, n_ctr, lambda n: departed(rcount.at[pl.ds(0, n)], rs_sem))

    w_total = sum((d + 1) * alike for d in range(pieces)) + (panels - 1) * owners

    def w_departed(own):
        departed(wcount.at[pl.ds(0, w_total - own)], w_sem)

    def unpack(g):
        for o in range(n_ctr):
            shard = head[o // wide_lanes, o % wide_lanes] // centers
            wpack[g, pl.ds(o, run, stride=n_ctr), :] = wrecv[shard, g].astype(F32)

    halves = solsend.shape[0]

    def so_copy(c_src, c_dst, h):
        at = c_src * halves + h
        return remote(solsend.at[h], solrecv.at[at], so_s.at[0], so_r.at[at], p_me, c_dst)

    def rh_copy(c_src, c_dst):
        at = lax.rem(c_src, owners)
        return remote(rhssend, rhsrecv.at[at], rh_s.at[lax.rem(c_dst, owners)], rh_r.at[at], p_me, c_dst)

    half_rows = own_rows // halves

    def send_solved(panel, h, result):
        sol_ref[:, h * half_rows:(h + 1) * half_rows] = result
        solsend[h] = result.astype(BF16)
        later = (panels - 1 - panel) * owners
        each(later, lambda k: so_copy(c_me, (panel + 1) * owners + k, h).start())

    def departed_so(n):
        ref = solrecv.at[pl.ds(0, n * halves)]
        remote(ref, ref, so_s.at[0], so_r.at[0], p_me, lax.rem(c_me + 1, n_ctr)).wait_send()

    def first_panel(d):
        arrived(wrecv.at[pl.ds(0, n_ctr - 1), pl.ds(0, d + 1)], w_sem)
        span_rows = panel_rows // (pieces * n_pts)
        parts = []
        for g in range(d + 1):
            unpack(g)
        for g in range(d + 1):
            turned = wpack[g].T.astype(BF16)
            parts += [turned[h * tcols:(h + 1) * tcols] for h in range(n_pts)]
        rhs = jnp.concatenate(parts, axis=1)
        for h in range(halves):
            rows_at = slice(h * half_rows, (h + 1) * half_rows)
            send_solved(0, h, dot_nt(rhs, pinv[rows_at, :(d + 1) * n_pts * span_rows]))
        if panels > 1:
            departed_so((panels - 1) * owners)
        w_departed(d + 1)

    for d in range(pieces):
        @pl.when((my_panel == 0) & (own_piece == d))
        def _():
            first_panel(d)

    for panel in range(1, panels):
        @pl.when(my_panel == panel)
        def _():
            done = panel * owners
            position = c_me - done
            arrived(wrecv.at[pl.ds(0, n_ctr - 1), pl.ds(0, 1)], w_sem)
            fac[...] = fac_raw[...].astype(BF16)
            unpack(own_piece)
            if fine:
                turned = wpack[own_piece].T
                own = jnp.concatenate([turned[h * tcols:(h + 1) * tcols] for h in range(n_pts)], axis=1)
            else:
                offset = position * own_rows
                part_len = panel_rows // n_pts
                within = pl.multiple_of(lax.rem(offset, part_len), own_rows)
                turned = wpack[0, pl.ds(within, own_rows), :].T
                for g in range(n_pts):
                    wblk[g] = turned[g * tcols:(g + 1) * tcols]
                own = wblk[offset // part_len]
            if fine:
                for b in range(done):
                    for h in range(halves):
                        so_copy(b, b, h).wait_recv()
                        begin = b * own_rows + h * half_rows
                        own = own - dot_nt(solrecv[b * halves + h], fac[:, begin:begin + half_rows])
            else:
                each(done, lambda k: so_copy(k, k, 0).wait_recv())
                solved = jnp.concatenate([solrecv[b] for b in range(done)], axis=1)
                own = own - dot_nt(solved, fac[:, :done * own_rows])
            rhssend[...] = own.astype(BF16)

            def below(k, fn):
                @pl.when(k > position if fine else k != position)
                def _():
                    fn(done + k)
            each(owners, lambda k: below(owners - 1 - k, lambda c: rh_copy(c_me, c).start()))
            if fine:
                acc[...] = jnp.zeros_like(acc)
                rhsrecv[position] = rhssend[...]
                for b in range(owners):
                    @pl.when(b <= position)
                    def _():
                        @pl.when(b < position)
                        def _():
                            rh_copy(done + b, done + b).wait_recv()
                        acc[...] += dot_nt(rhsrecv[b], pinv[:, b * own_rows:(b + 1) * own_rows])
                result = acc[...]
            else:
                rhsrecv[position] = rhssend[...]
                each(owners, lambda k: below(k, lambda c: rh_copy(c, c).wait_recv()))
                result = dot_nt(jnp.concatenate([rhsrecv[b] for b in range(owners)], axis=1), pinv[...])
            later = (panels - 1 - panel) * owners
            if later:
                for h in range(halves):
                    send_solved(panel, h, result[:, h * half_rows:(h + 1) * half_rows])
                departed_so(later)
            else:
                sol_ref[...] = result
            each(owners, lambda k: below(k, lambda c: rh_copy(c_me, c).wait_send()))
            w_departed(1)


def emit(grad_ref, sol_ref, grad_out, sol_out, sem):
    first = pltpu.make_async_copy(grad_ref, grad_out, sem.at[0])
    second = pltpu.make_async_copy(sol_ref, sol_out, sem.at[1])
    first.start()
    second.start()
    first.wait()
    second.wait()


def body(
    points, point_class, targets, class_weight, inv_scale, centers, coefficients, center_index, factor, panel_inverse
):
    n_pts, n_ctr = lax.axis_size("pts"), lax.axis_size("ctr")
    rows, feats = points.shape
    n_cen, n_tgt = coefficients.shape
    tcols = n_tgt // n_pts
    own_rows, panel_rows = panel_inverse.shape
    panels = factor.shape[1] // panel_rows
    owners = panel_rows // own_rows
    total = rows * n_pts * n_ctr
    group = rows * n_ctr
    per_block = LANES // rows
    pt_blocks = n_ctr // per_block
    blocks = n_pts * pt_blocks
    slots = center_index.shape[0] // n_ctr
    pieces = owners if own_rows % LANES == 0 else 1
    halves = 1
    run = slots // panels // pieces // n_pts
    w_most = pieces * (pieces + 1) // 2 * (owners // pieces) + (panels - 1) * owners
    solved_cols = panel_rows * (panels - 1)
    chunk = 1024
    index = center_index.reshape(-1, LANES)
    vmem = pl.BlockSpec(memory_space=pltpu.VMEM)
    hbm = pl.BlockSpec(memory_space=pltpu.HBM)
    dma = pltpu.SemaphoreType.DMA
    scratch = [
        pltpu.VMEM((rows, feats), BF16),
        pltpu.VMEM((1, rows), jnp.int32),
        pltpu.VMEM((rows, n_tgt), F32),
        pltpu.SMEM((1, class_weight.shape[0]), F32),
        pltpu.VMEM((1, feats), F32),
        pltpu.VMEM(index.shape, jnp.int32),
        pltpu.SMEM((8, LANES), jnp.int32),
        pltpu.VMEM((n_cen, feats), BF16),
        pltpu.VMEM((n_cen, n_tgt), BF16),
        pltpu.VMEM((own_rows, panel_rows), F32),
        pltpu.VMEM((own_rows, panel_rows), BF16),
        pltpu.VMEM((own_rows, solved_cols), F32),
        pltpu.VMEM((own_rows, solved_cols), BF16),
        pltpu.VMEM((8, n_cen), F32),
        pltpu.VMEM((total, LANES), F32),
        pltpu.VMEM((total, feats), BF16),
        pltpu.VMEM((total, n_cen), BF16),
        pltpu.VMEM((slots, total), BF16),
        pltpu.VMEM((slots, feats), F32),
        pltpu.VMEM((group, n_tgt), F32),
        pltpu.VMEM((blocks, tcols, LANES), F32),
        pltpu.VMEM((n_ctr, tcols, LANES), F32),
        pltpu.VMEM((8, LANES), F32),
        pltpu.VMEM((per_block, 8, LANES), F32),
        pltpu.VMEM((tcols, LANES), BF16),
        pltpu.VMEM((blocks, tcols, LANES), BF16),
        pltpu.VMEM((n_ctr, tcols, LANES), BF16),
        pltpu.VMEM((panels, pieces, run, n_tgt), BF16),
        pltpu.VMEM((n_ctr, pieces, run, n_tgt), BF16),
        pltpu.VMEM((w_most, run, n_tgt), BF16),
        pltpu.VMEM((pieces, run * n_ctr, n_tgt), F32),
        pltpu.VMEM((n_pts, tcols, own_rows), F32),
        pltpu.VMEM((halves, tcols, own_rows // halves), BF16),
        pltpu.VMEM((owners * (panels - 1) * halves, tcols, own_rows // halves), BF16),
        pltpu.VMEM((tcols, own_rows), BF16),
        pltpu.VMEM((owners, tcols, own_rows), BF16),
        pltpu.VMEM((tcols, own_rows), F32),
        dma((10,)), dma((n_cen // chunk,)),
        dma((2,)), dma((2,)), dma((2,)), dma((2,)), dma((2,)), dma((2,)),
        dma((1,)), dma((owners * (panels - 1) * halves,)),
        dma((owners,)), dma((owners,)),
    ]
    grad, solved = pl.pallas_call(
        functools.partial(kernel, n_pts, n_ctr, panels, chunk, 512),
        out_shape=(
            pltpu.VMEM((tcols, n_cen), F32),
            pltpu.VMEM((tcols, own_rows), F32),
        ),
        in_specs=[hbm] * 10,
        out_specs=(vmem, vmem),
        scratch_shapes=scratch,
        compiler_params=pltpu.CompilerParams(
            collective_id=0, has_side_effects=True, vmem_limit_bytes=60000000
        ),
        name="falkon",
    )(
        points, point_class[None, :], targets, class_weight[None, :], inv_scale[None, :],
        index, centers, coefficients, factor, panel_inverse,
    )
    grad, solved = pl.pallas_call(
        emit,
        out_shape=(
            jax.ShapeDtypeStruct((tcols, n_cen), F32),
            jax.ShapeDtypeStruct((tcols, own_rows), F32),
        ),
        in_specs=[vmem, vmem],
        out_specs=(hbm, hbm),
        scratch_shapes=[dma((2,))],
        compiler_params=pltpu.CompilerParams(vmem_limit_bytes=1048576),
        name="emit",
    )(grad, solved)
    return grad.T, solved.T


def solution(mesh):
    placed = (
        P(("pts", "ctr"), None),
        P(("pts", "ctr")),
        P(("pts", "ctr"), None),
        P(),
        P(),
        P("ctr", None),
        P("ctr", None),
        P(),
        P("ctr", None),
        P("ctr", None),
    )
    return jax.shard_map(
        body,
        mesh=mesh,
        in_specs=placed,
        out_specs=(P("ctr", "pts"), P("ctr", "pts")),
        check_vma=False,
    )
```

```python
import functools

import jax
import jax.numpy as jnp
from jax import lax
from jax.experimental import pallas as pl
from jax.experimental.pallas import tpu as pltpu
from jax.sharding import PartitionSpec as P

MESH = pl.DeviceIdType.MESH
NT = (((1,), (1,)), ((), ()))
F32 = jnp.float32
BF16 = jnp.bfloat16
LANES = 128


def dot_nt(left, right):
    return lax.dot_general(left, right, NT, preferred_element_type=F32)


def iota(shape, dim):
    return lax.broadcasted_iota(jnp.int32, shape, dim)


def hot(mask):
    return jnp.where(mask, 1.0, 0.0).astype(BF16)


def half_norm(x):
    return 0.5 * jnp.sum(jnp.square(x.astype(F32)), axis=1, keepdims=True)


def half_norm_row(x):
    square = jnp.square(x.astype(F32))
    folded = square[:, :LANES]
    for begin in range(LANES, square.shape[1], LANES):
        folded = folded + square[:, begin:begin + LANES]
    return 0.5 * jnp.sum(folded.T, axis=0, keepdims=True)


def each(n, fn):
    def step(k, carry):
        fn(k)
        return carry
    lax.fori_loop(0, n, step, 0)


def unrolled(n, fn):
    if n > 8:
        return each(n, fn)
    for k in range(n):
        fn(k)


def kernel(
    n_pts, n_ctr, panels, chunk, sub,
    pts_hbm, cls_hbm, tgt_hbm, cw_hbm, inv_hbm, idx_hbm, cen_hbm, coef_hbm, fac_hbm, pinv_hbm,
    grad_ref, sol_ref,
    pts, cls, tgt, cw, inv_row, idx, head,
    cen, coef, pinv_raw, pinv, fac_raw, fac, rnorm, pnorm, pall, kmat, ksel,
    sel, total_acc, part, part_recv, wt_send, wt_recv, rsend, rbuf, rcount,
    wsend, wrecv, wcount, wsend_t, wrecv_t, tall, mixed, wpack, wblk, solsend, solrecv, rhssend, rhsrecv, acc,
    loc, cen_sem, pt_sem, fw_sem, pr_sem, wt_sem, rs_sem, w0_sem, w_sem, so_s, so_r, rh_s, rh_r,
):
    p_me, c_me = lax.axis_index("pts"), lax.axis_index("ctr")
    rows, feats = pts.shape
    group = rows * n_ctr
    centers = cen.shape[0]
    targets = tgt.shape[1]
    tcols = targets // n_pts
    own_rows, panel_rows = pinv.shape
    owners = panel_rows // own_rows
    my_panel = c_me // owners
    chunks = centers // chunk
    blocks = rbuf.shape[0]
    pt_blocks = blocks // n_pts
    per_block = n_ctr // pt_blocks
    width = rows * per_block
    me = p_me * n_ctr + c_me
    first_red = (n_ctr - blocks) // 2
    reduces = (c_me >= first_red) & (c_me < first_red + blocks)
    blk = jnp.where(reduces, c_me - first_red, 0)
    blk_pts = lax.rem(blk + p_me // 2 * 2, n_pts)
    own_block = reduces & (blk_pts == p_me)

    def remote(src, dst, send, recv, p, c):
        return pltpu.make_async_remote_copy(
            src_ref=src, dst_ref=dst, send_sem=send, recv_sem=recv,
            device_id={"pts": p, "ctr": c}, device_id_type=MESH,
        )

    def arrived(ref, sem):
        remote(ref, ref, sem.at[0], sem.at[1], p_me, lax.rem(c_me + 1, n_ctr)).wait_recv()

    def departed(ref, sem):
        remote(ref, ref, sem.at[0], sem.at[1], p_me, lax.rem(c_me + 1, n_ctr)).wait_send()

    def unless(flag, most, fn):
        @pl.when(flag)
        def _():
            fn(most - 1)

        @pl.when(jnp.logical_not(flag))
        def _():
            fn(most)

    def local(src, dst, k):
        return pltpu.make_async_copy(src, dst, loc.at[k])

    def cen_copy(k):
        at = pl.ds(pl.multiple_of(k * chunk, chunk), chunk)
        return pltpu.make_async_copy(cen_hbm.at[at], cen.at[at], cen_sem.at[k])

    pts_copy = local(pts_hbm, pts, 0)
    inv_copy = local(inv_hbm, inv_row, 1)
    cls_copy = local(cls_hbm, cls, 2)
    cw_copy = local(cw_hbm, cw, 3)
    tgt_copy = local(tgt_hbm, tgt, 4)
    idx_copy = local(idx_hbm, idx, 5)
    head_copy = local(idx_hbm.at[pl.ds(0, head.shape[0])], head, 6)
    coef_copy = local(coef_hbm, coef, 7)
    pinv_copy = local(pinv_hbm, pinv_raw, 8)
    fac_copy = local(fac_hbm.at[:, pl.ds(0, fac.shape[1])], fac_raw, 9)
    pts_copy.start()
    inv_copy.start()

    barrier = pltpu.get_barrier_semaphore()

    def peer(k):
        above = n_ctr - 1 - c_me
        low = jnp.where(k < above, n_ctr - 1 - k, k - above)
        high = jnp.where(k < c_me, k, n_ctr - 1 - k + c_me)
        return jnp.where(c_me < above, low, high)
    pair = p_me // 2 * 2

    def mate(k):
        return 2 * pair + 1 - p_me if k == 0 else lax.rem(pair + k + 1, n_pts)

    def greet(p, c):
        pl.semaphore_signal(barrier, inc=1, device_id={"pts": p, "ctr": c}, device_id_type=MESH)

    each(n_ctr - 1, lambda k: greet(p_me, peer(k)))
    for k in range(n_pts - 1):
        greet(mate(k), c_me)

    cls_copy.start()
    cw_copy.start()
    each(chunks, lambda k: cen_copy(k).start())
    idx_copy.start()
    tgt_copy.start()
    head_copy.start()
    coef_copy.start()

    pts_copy.wait()
    inv_copy.wait()
    inv = inv_row[...]
    own_slot = pl.ds(pl.multiple_of(me * rows, rows), rows)
    pall[own_slot, :] = (pts[...].astype(F32) * inv).astype(BF16)
    pl.semaphore_wait(barrier, n_ctr + n_pts - 2)

    def pt_copy(c_src, c_dst):
        slot = pl.ds(pl.multiple_of((p_me * n_ctr + c_src) * rows, rows), rows)
        return remote(pall.at[slot], pall.at[slot], pt_sem.at[0], pt_sem.at[1], p_me, c_dst)
    each(n_ctr - 1, lambda k: pt_copy(c_me, peer(k)).start())

    cls_copy.wait()
    cw_copy.wait()
    lane_of = lax.rem(c_me, per_block) * rows
    place = hot(iota((rows, width), 1) == iota((rows, width), 0) + lane_of)
    label = jnp.dot(
        jnp.broadcast_to(cls[...].astype(F32).astype(BF16), (8, rows)), place, preferred_element_type=F32
    )
    mine_lane = (iota((8, width), 1) >= lane_of) & (iota((8, width), 1) < lane_of + rows)
    weight = jnp.zeros((8, width), F32)
    for k in range(cw.shape[1]):
        weight = jnp.where(mine_lane & (label == float(k)), cw[0, k], weight)
    wt_send[...] = weight

    def wt_dest(k):
        return first_red + c_me // per_block * n_pts + k

    def wt_copy(c_src, c_dst):
        at = lax.rem(c_src, per_block)
        return remote(wt_send, wt_recv.at[at], wt_sem.at[0], wt_sem.at[1], p_me, c_dst)

    def not_me(c, fn):
        @pl.when(c != c_me)
        def _():
            fn(c)
    each(n_pts, lambda k: not_me(wt_dest(k), lambda c: wt_copy(c_me, c).start()))

    own_weights = reduces & (c_me // per_block == blk // n_pts)

    @pl.when(own_weights)
    def _():
        wt_recv[lax.rem(c_me, per_block)] = weight

    step = 256

    def scale(k):
        at = pl.ds(pl.multiple_of(k * step, step), step)
        scaled = (cen[at, :].astype(F32) * inv).astype(BF16)
        cen[at, :] = scaled
        rnorm[0:1, at] = half_norm_row(scaled)

    def scale_chunk(k):
        cen_copy(k).wait()
        unrolled(chunk // step, lambda j: scale(k * (chunk // step) + j))
    each(chunks, scale_chunk)

    idx_copy.wait()
    shift, wide_lanes = 64, idx.shape[1]
    per = wide_lanes // n_ctr
    slots = sel.shape[0]
    relative = idx[...] - c_me * centers
    relative = jnp.where((relative >= 0) & (relative < centers), relative, 0)
    fold = hot(iota((wide_lanes, wide_lanes), 0) // n_ctr == iota((wide_lanes, wide_lanes), 1))
    spread = hot(iota((slots, relative.shape[0]), 0) // per == iota((slots, relative.shape[0]), 1))

    def column(value):
        folded = jnp.dot(value.astype(F32).astype(BF16), fold, preferred_element_type=F32)
        return jnp.dot(spread, folded.astype(BF16), preferred_element_type=F32)
    both = shift * column(relative // shift) + column(lax.rem(relative, shift))
    at_lane = lax.rem(iota((slots, wide_lanes), 0), per) == iota((slots, wide_lanes), 1)
    local_row = jnp.sum(jnp.where(at_lane, both, 0.0), axis=1, keepdims=True).astype(jnp.int32)
    coef_copy.wait()
    tgt_copy.wait()
    head_copy.wait()
    pinv_copy.start()
    fac_copy.start()

    arrived(pall.at[pl.ds(0, (n_ctr - 1) * rows)], pt_sem)

    def group_at(p):
        return pl.ds(pl.multiple_of(p * group, group), group)

    def fw_copy(p_src, p_dst):
        at = group_at(p_src)
        return remote(pall.at[at], pall.at[at], fw_sem.at[0], fw_sem.at[1], p_dst, c_me)
    for k in range(n_pts - 1):
        fw_copy(p_me, mate(k)).start()

    def sub_at(k, j):
        return pl.ds(pl.multiple_of(k * chunk + j * sub, sub), sub)

    def kernel_block(left, norm, at):
        return jnp.exp(dot_nt(left, cen[at, :]) - norm - rnorm[0:1, at]).astype(BF16)
    mine = pall[group_at(p_me), :]
    mine_norm = half_norm(mine)
    pnorm[group_at(p_me), :] = jnp.broadcast_to(mine_norm, (group, LANES))
    total = jnp.zeros((group, targets), F32)
    saved = []
    for k in range(chunks):
        at = pl.ds(k * chunk, chunk)
        block = kernel_block(mine, mine_norm, at)
        kmat[group_at(p_me), at] = block
        if group > LANES:
            total = total + jnp.dot(block, coef[at, :], preferred_element_type=F32)
        else:
            saved.append((block, at))
    for block, at in saved:
        total = total + jnp.dot(block, coef[at, :], preferred_element_type=F32)
    total_acc[...] = total
    own_rows_at = pl.ds(pl.multiple_of(c_me * rows, rows), rows)
    total_acc[own_rows_at, :] = total_acc[own_rows_at, :] - tgt[...]
    for b in range(pt_blocks):
        turned = total_acc[b * width:(b + 1) * width, :].T
        for q in range(n_pts):
            part[b * n_pts + q] = turned[q * tcols:(q + 1) * tcols]

    def part_of(b):
        return b // n_pts * n_pts + lax.rem(b + p_me // 2 * 2, n_pts)

    def pr_copy(c_src, c_dst):
        return remote(
            part.at[part_of(c_dst - first_red)], part_recv.at[c_src], pr_sem.at[0], pr_sem.at[1], p_me, c_dst
        )
    def pr_dest(k):
        return jnp.where(c_me < n_ctr // 2, first_red + blocks - 1 - k, first_red + k)
    each(blocks, lambda k: not_me(pr_dest(k), lambda c: pr_copy(c_me, c).start()))
    part_recv[c_me] = part[part_of(blk)]

    sel[...] = jnp.zeros_like(sel)

    def select(k):
        at = pl.ds(pl.multiple_of(k * chunk, chunk), chunk)
        picked = hot(iota((slots, chunk), 1) == local_row - k * chunk)
        return jnp.dot(picked, cen[at, :], preferred_element_type=F32)
    sel[...] = functools.reduce(lambda a, k: a + select(k), range(1, chunks), select(0))

    arrived(pall.at[pl.ds(0, (n_pts - 1) * group)], fw_sem)

    def rs_slot(p, b):
        return p * pt_blocks + b

    def rs_copy(c_dst):
        at = rs_slot(p_me, blk // n_pts)
        return remote(rsend, rbuf.at[at], rs_sem.at[0], rs_sem.at[1], blk_pts, c_dst)

    @pl.when(reduces)
    def _():
        unless(own_weights, per_block, lambda n: arrived(wt_recv.at[pl.ds(0, n)], wt_sem))
        weights = jnp.sum(wt_recv[...], axis=0)[0:1]
        arrived(part_recv.at[pl.ds(0, n_ctr - 1)], pr_sem)
        residual = (weights * jnp.sum(part_recv[...], axis=0)).astype(BF16)
        rsend[...] = residual

        @pl.when(own_block)
        def _():
            rbuf[rs_slot(p_me, blk // n_pts)] = residual
            each(n_ctr - 1, lambda k: rs_copy(peer(k)).start())

        @pl.when(jnp.logical_not(own_block))
        def _():
            each(n_ctr - 1, lambda k: rs_copy(peer(k)).start())
            rs_copy(c_me).start()

    together = n_pts - 1 if group * n_pts <= 512 else 1
    for first in range(0, n_pts - 1, together):
        mates = [mate(k) for k in range(first, first + together)]
        left = jnp.concatenate([pall[group_at(p), :] for p in mates], axis=0)
        left_norm = half_norm(left)
        for k, p in enumerate(mates):
            pnorm[group_at(p), :] = jnp.broadcast_to(left_norm[k * group:(k + 1) * group], (group, LANES))

        def fill(k):
            for j in range(chunk // sub):
                at = sub_at(k, j)
                block = kernel_block(left, left_norm, at)
                for n, p in enumerate(mates):
                    kmat[group_at(p), at] = block[n * group:(n + 1) * group]
        unrolled(chunks, fill)

    chosen = sel[...].astype(BF16)
    chosen_norm = half_norm(chosen)
    span = 512

    def window_kernel(k):
        at = pl.ds(pl.multiple_of(k * span, span), span)
        norm = pnorm[at, :].T[0:1]
        ksel[:, at] = jnp.exp(dot_nt(chosen, pall[at, :]) - norm - chosen_norm).astype(BF16)
    each(pall.shape[0] // span, window_kernel)

    unless(own_block, blocks, lambda n: arrived(rbuf.at[pl.ds(0, n)], rs_sem))

    wide_t = jnp.concatenate([rbuf[b] for b in range(blocks)], axis=1)
    tall_t = jnp.concatenate([wide_t] * n_pts, axis=0)
    pieces, run = wsend.shape[1], wsend.shape[2]
    fine = pieces > 1
    lane_group = iota((run, targets), 1) // tcols
    per_panel = slots // panels

    def pack(panel):
        window = dot_nt(ksel[panel * per_panel:(panel + 1) * per_panel], tall_t)
        for g in range(pieces):
            packed = jnp.zeros((run, targets), F32)
            for h in range(n_pts):
                begin = (g * n_pts + h) * run
                packed = packed + jnp.where(lane_group == h, window[begin:begin + run], 0.0)
            wsend[panel, g] = packed.astype(BF16)
    own_piece = lax.rem(c_me, owners) * pieces // owners

    def w_first(d, c_dst):
        return remote(
            wsend.at[0, pl.ds(0, d + 1)], wrecv.at[c_me, pl.ds(0, d + 1)], w_sem.at[0], w_sem.at[1], p_me, c_dst
        )

    def w_later(c_dst):
        d = lax.rem(c_dst, owners) * pieces // owners
        return remote(
            wsend.at[c_dst // owners, pl.ds(d, 1)], wrecv.at[c_me, pl.ds(d, 1)], w_sem.at[0], w_sem.at[1], p_me, c_dst
        )
    alike = owners // pieces
    lane_parts = wsend_t.shape[0]

    def reach(d):
        return ((d + 1) * lane_parts + pieces - 1) // pieces

    def wt_first(d, c_src, c_dst):
        at = pl.ds(0, reach(d))
        return remote(wsend_t.at[at], wrecv_t.at[c_src, at], w0_sem.at[0], w0_sem.at[1 + c_src], p_me, c_dst)
    if fine:
        turned = dot_nt(wide_t, ksel[:per_panel]).astype(BF16)
        for g in range(lane_parts):
            wsend_t[g] = turned[:, g * LANES:(g + 1) * LANES]
    else:
        pack(0)
    for d in range(pieces):
        send = functools.partial(wt_first, d, c_me) if fine else functools.partial(w_first, d)
        each(alike, lambda j: not_me(d * alike + j, lambda c: send(c).start()))
    if fine:
        wrecv_t[c_me] = wsend_t[...]
    for panel in range(1, panels):
        pack(panel)
    each((panels - 1) * owners, lambda j: not_me(owners + j, lambda c: w_later(c).start()))
    if not fine:
        wrecv[c_me] = wsend[my_panel]
    else:
        @pl.when(my_panel > 0)
        def _():
            wrecv[c_me] = wsend[my_panel]

    def backward(k):
        at = pl.ds(pl.multiple_of(k * chunk, chunk), chunk)
        grad_ref[:, at] = jnp.dot(wide_t, kmat[:, at], preferred_element_type=F32)
    unrolled(chunks, backward)
    pinv_copy.wait()
    fac_copy.wait()
    if fine:
        @pl.when(my_panel > 0)
        def _():
            pinv[...] = pinv_raw[...].astype(BF16)

        @pl.when(my_panel == 0)
        def _():
            for g in range(own_rows // LANES):
                rows_at = slice(g * LANES, (g + 1) * LANES)
                for begin in range(0, panel_rows, LANES):
                    tall[g, begin:begin + LANES] = pinv_raw[rows_at, begin:begin + LANES].T
                for o in range(n_ctr):
                    mixed[o, :, rows_at] = tall[g, pl.ds(o, per_panel, stride=n_ctr), :].astype(BF16)
    else:
        pinv[...] = pinv_raw[...].astype(BF16)

    departed(pall.at[pl.ds(0, (n_ctr - 1) * rows)], pt_sem)
    unless(own_weights, n_pts, lambda n: departed(wt_recv.at[pl.ds(0, n)], wt_sem))
    departed(pall.at[pl.ds(0, (n_pts - 1) * group)], fw_sem)
    unless(reduces, blocks, lambda n: departed(part.at[pl.ds(0, n)], pr_sem))

    @pl.when(reduces)
    def _():
        unless(own_block, n_ctr, lambda n: departed(rcount.at[pl.ds(0, n)], rs_sem))

    w_ahead = sum((d + 1) * alike for d in range(pieces))
    w_after = (panels - 1) * owners

    def w_departed(own, panel):
        if fine:
            departed(rcount.at[pl.ds(0, sum(reach(d) for d in range(pieces)) - (reach(own) if panel == 0 else 0))], w0_sem)
            departed(wcount.at[pl.ds(0, w_after - (panel > 0))], w_sem)
        else:
            departed(wcount.at[pl.ds(0, w_ahead + w_after - (own + 1 if panel == 0 else 1))], w_sem)

    def unpack(g):
        for o in range(n_ctr):
            shard = head[o // wide_lanes, o % wide_lanes] // centers
            wpack[g, pl.ds(o, run, stride=n_ctr), :] = wrecv[shard, g].astype(F32)

    halves = solsend.shape[0]

    def so_copy(c_src, c_dst, h):
        at = c_src * halves + h
        return remote(solsend.at[h], solrecv.at[at], so_s.at[0], so_r.at[at], p_me, c_dst)

    def rh_copy(c_src, c_dst):
        at = lax.rem(c_src, owners)
        return remote(rhssend, rhsrecv.at[at], rh_s.at[lax.rem(c_dst, owners)], rh_r.at[at], p_me, c_dst)

    half_rows = own_rows // halves

    def send_solved(panel, h, result):
        sol_ref[:, h * half_rows:(h + 1) * half_rows] = result
        solsend[h] = result.astype(BF16)
        later = (panels - 1 - panel) * owners
        each(later, lambda k: so_copy(c_me, (panel + 1) * owners + k, h).start())

    def departed_so(n):
        ref = solrecv.at[pl.ds(0, n * halves)]
        remote(ref, ref, so_s.at[0], so_r.at[0], p_me, lax.rem(c_me + 1, n_ctr)).wait_send()

    def first_panel(d):
        if fine:
            depth = reach(d) * LANES
            result = jnp.zeros((tcols, own_rows), F32)
            for k in range(n_ctr - 1, -1, -1):
                source = c_me if k == n_ctr - 1 else peer(k)
                if k < n_ctr - 1:
                    wt_first(d, source, source).wait_recv()
                spot = 0
                for o in range(1, n_ctr):
                    spot = jnp.where(head[o // wide_lanes, o % wide_lanes] // centers == source, o, spot)
                left = jnp.concatenate([wrecv_t[source, g] for g in range(reach(d))], axis=1)
                result = result + jnp.dot(left, mixed[spot, :depth], preferred_element_type=F32)
            send_solved(0, 0, result)
        else:
            arrived(wrecv.at[pl.ds(0, n_ctr - 1), pl.ds(0, d + 1)], w_sem)
            for g in range(d + 1):
                unpack(g)
            parts = []
            for g in range(d + 1):
                turned = wpack[g].T.astype(BF16)
                parts += [turned[h * tcols:(h + 1) * tcols] for h in range(n_pts)]
            rhs = jnp.concatenate(parts, axis=1)
            send_solved(0, 0, dot_nt(rhs, pinv[:, :(d + 1) * (panel_rows // pieces)]))
        if panels > 1:
            departed_so((panels - 1) * owners)
        w_departed(d, 0)

    for d in range(pieces):
        @pl.when((my_panel == 0) & (own_piece == d))
        def _():
            first_panel(d)

    for panel in range(1, panels):
        @pl.when(my_panel == panel)
        def _():
            done = panel * owners
            position = c_me - done
            arrived(wrecv.at[pl.ds(0, n_ctr - 1), pl.ds(0, 1)], w_sem)
            fac[...] = fac_raw[...].astype(BF16)
            unpack(own_piece)
            if fine:
                turned = wpack[own_piece].T
                own = jnp.concatenate([turned[h * tcols:(h + 1) * tcols] for h in range(n_pts)], axis=1)
            else:
                offset = position * own_rows
                part_len = panel_rows // n_pts
                within = pl.multiple_of(lax.rem(offset, part_len), own_rows)
                turned = wpack[0, pl.ds(within, own_rows), :].T
                for g in range(n_pts):
                    wblk[g] = turned[g * tcols:(g + 1) * tcols]
                own = wblk[offset // part_len]
            if fine:
                for b in range(done):
                    for h in range(halves):
                        so_copy(b, b, h).wait_recv()
                        begin = b * own_rows + h * half_rows
                        own = own - dot_nt(solrecv[b * halves + h], fac[:, begin:begin + half_rows])
            else:
                each(done, lambda k: so_copy(k, k, 0).wait_recv())
                solved = jnp.concatenate([solrecv[b] for b in range(done)], axis=1)
                own = own - dot_nt(solved, fac[:, :done * own_rows])
            rhssend[...] = own.astype(BF16)

            def below(k, fn):
                @pl.when(k > position if fine else k != position)
                def _():
                    fn(done + k)
            each(owners, lambda k: below(owners - 1 - k, lambda c: rh_copy(c_me, c).start()))
            if fine:
                acc[...] = jnp.zeros_like(acc)
                rhsrecv[position] = rhssend[...]
                for b in range(owners):
                    @pl.when(b <= position)
                    def _():
                        @pl.when(b < position)
                        def _():
                            rh_copy(done + b, done + b).wait_recv()
                        acc[...] += dot_nt(rhsrecv[b], pinv[:, b * own_rows:(b + 1) * own_rows])
                result = acc[...]
            else:
                rhsrecv[position] = rhssend[...]
                each(owners, lambda k: below(k, lambda c: rh_copy(c, c).wait_recv()))
                result = dot_nt(jnp.concatenate([rhsrecv[b] for b in range(owners)], axis=1), pinv[...])
            later = (panels - 1 - panel) * owners
            if later:
                for h in range(halves):
                    send_solved(panel, h, result[:, h * half_rows:(h + 1) * half_rows])
                departed_so(later)
            else:
                sol_ref[...] = result
            each(owners, lambda k: below(k, lambda c: rh_copy(c_me, c).wait_send()))
            w_departed(0, panel)


def emit(grad_ref, sol_ref, grad_out, sol_out, sem):
    first = pltpu.make_async_copy(grad_ref, grad_out, sem.at[0])
    second = pltpu.make_async_copy(sol_ref, sol_out, sem.at[1])
    first.start()
    second.start()
    first.wait()
    second.wait()


def body(
    points, point_class, targets, class_weight, inv_scale, centers, coefficients, center_index, factor, panel_inverse
):
    n_pts, n_ctr = lax.axis_size("pts"), lax.axis_size("ctr")
    rows, feats = points.shape
    n_cen, n_tgt = coefficients.shape
    tcols = n_tgt // n_pts
    own_rows, panel_rows = panel_inverse.shape
    panels = factor.shape[1] // panel_rows
    owners = panel_rows // own_rows
    total = rows * n_pts * n_ctr
    group = rows * n_ctr
    per_block = LANES // rows
    pt_blocks = n_ctr // per_block
    blocks = n_pts * pt_blocks
    slots = center_index.shape[0] // n_ctr
    pieces = owners if own_rows % LANES == 0 else 1
    halves = 1
    lane_parts = max(1, slots // panels // LANES)
    run = slots // panels // pieces // n_pts
    w_most = pieces * (pieces + 1) // 2 * (owners // pieces) + (panels - 1) * owners
    solved_cols = panel_rows * (panels - 1)
    chunk = 1024
    index = center_index.reshape(-1, LANES)
    vmem = pl.BlockSpec(memory_space=pltpu.VMEM)
    hbm = pl.BlockSpec(memory_space=pltpu.HBM)
    dma = pltpu.SemaphoreType.DMA
    scratch = [
        pltpu.VMEM((rows, feats), BF16),
        pltpu.VMEM((1, rows), jnp.int32),
        pltpu.VMEM((rows, n_tgt), F32),
        pltpu.SMEM((1, class_weight.shape[0]), F32),
        pltpu.VMEM((1, feats), F32),
        pltpu.VMEM(index.shape, jnp.int32),
        pltpu.SMEM((8, LANES), jnp.int32),
        pltpu.VMEM((n_cen, feats), BF16),
        pltpu.VMEM((n_cen, n_tgt), BF16),
        pltpu.VMEM((own_rows, panel_rows), F32),
        pltpu.VMEM((own_rows, panel_rows), BF16),
        pltpu.VMEM((own_rows, solved_cols), F32),
        pltpu.VMEM((own_rows, solved_cols), BF16),
        pltpu.VMEM((8, n_cen), F32),
        pltpu.VMEM((total, LANES), F32),
        pltpu.VMEM((total, feats), BF16),
        pltpu.VMEM((total, n_cen), BF16),
        pltpu.VMEM((slots, total), BF16),
        pltpu.VMEM((slots, feats), F32),
        pltpu.VMEM((group, n_tgt), F32),
        pltpu.VMEM((blocks, tcols, LANES), F32),
        pltpu.VMEM((n_ctr, tcols, LANES), F32),
        pltpu.VMEM((8, LANES), F32),
        pltpu.VMEM((per_block, 8, LANES), F32),
        pltpu.VMEM((tcols, LANES), BF16),
        pltpu.VMEM((blocks, tcols, LANES), BF16),
        pltpu.VMEM((n_ctr, tcols, LANES), BF16),
        pltpu.VMEM((panels, pieces, run, n_tgt), BF16),
        pltpu.VMEM((n_ctr, pieces, run, n_tgt), BF16),
        pltpu.VMEM((w_most, run, n_tgt), BF16),
        pltpu.VMEM((lane_parts, tcols, LANES), BF16),
        pltpu.VMEM((n_ctr, lane_parts, tcols, LANES), BF16),
        pltpu.VMEM((max(1, own_rows // LANES), panel_rows, LANES), F32),
        pltpu.VMEM((n_ctr, slots // panels, own_rows), BF16),
        pltpu.VMEM((pieces, run * n_ctr, n_tgt), F32),
        pltpu.VMEM((n_pts, tcols, own_rows), F32),
        pltpu.VMEM((halves, tcols, own_rows // halves), BF16),
        pltpu.VMEM((owners * (panels - 1) * halves, tcols, own_rows // halves), BF16),
        pltpu.VMEM((tcols, own_rows), BF16),
        pltpu.VMEM((owners, tcols, own_rows), BF16),
        pltpu.VMEM((tcols, own_rows), F32),
        dma((10,)), dma((n_cen // chunk,)),
        dma((2,)), dma((2,)), dma((2,)), dma((2,)), dma((2,)), dma((1 + n_ctr,)), dma((2,)),
        dma((1,)), dma((owners * (panels - 1) * halves,)),
        dma((owners,)), dma((owners,)),
    ]
    grad, solved = pl.pallas_call(
        functools.partial(kernel, n_pts, n_ctr, panels, chunk, 512),
        out_shape=(
            pltpu.VMEM((tcols, n_cen), F32),
            pltpu.VMEM((tcols, own_rows), F32),
        ),
        in_specs=[hbm] * 10,
        out_specs=(vmem, vmem),
        scratch_shapes=scratch,
        compiler_params=pltpu.CompilerParams(
            collective_id=0, has_side_effects=True, vmem_limit_bytes=60000000
        ),
        name="falkon",
    )(
        points, point_class[None, :], targets, class_weight[None, :], inv_scale[None, :],
        index, centers, coefficients, factor, panel_inverse,
    )
    grad, solved = pl.pallas_call(
        emit,
        out_shape=(
            jax.ShapeDtypeStruct((tcols, n_cen), F32),
            jax.ShapeDtypeStruct((tcols, own_rows), F32),
        ),
        in_specs=[vmem, vmem],
        out_specs=(hbm, hbm),
        scratch_shapes=[dma((2,))],
        compiler_params=pltpu.CompilerParams(vmem_limit_bytes=1048576),
        name="emit",
    )(grad, solved)
    return grad.T, solved.T


def solution(mesh):
    placed = (
        P(("pts", "ctr"), None),
        P(("pts", "ctr")),
        P(("pts", "ctr"), None),
        P(),
        P(),
        P("ctr", None),
        P("ctr", None),
        P(),
        P("ctr", None),
        P("ctr", None),
    )
    return jax.shard_map(
        body,
        mesh=mesh,
        in_specs=placed,
        out_specs=(P("ctr", "pts"), P("ctr", "pts")),
        check_vma=False,
    )
```

```python
import functools

import jax
import jax.numpy as jnp
from jax import lax
from jax.experimental import pallas as pl
from jax.experimental.pallas import tpu as pltpu
from jax.sharding import PartitionSpec as P

MESH = pl.DeviceIdType.MESH
NT = (((1,), (1,)), ((), ()))
F32 = jnp.float32
BF16 = jnp.bfloat16
LANES = 128


def dot_nt(left, right):
    return lax.dot_general(left, right, NT, preferred_element_type=F32)


def iota(shape, dim):
    return lax.broadcasted_iota(jnp.int32, shape, dim)


def hot(mask):
    return jnp.where(mask, 1.0, 0.0).astype(BF16)


def half_norm(x):
    return 0.5 * jnp.sum(jnp.square(x.astype(F32)), axis=1, keepdims=True)


def half_norm_row(x):
    square = jnp.square(x.astype(F32))
    folded = square[:, :LANES]
    for begin in range(LANES, square.shape[1], LANES):
        folded = folded + square[:, begin:begin + LANES]
    return 0.5 * jnp.sum(folded.T, axis=0, keepdims=True)


def each(n, fn):
    def step(k, carry):
        fn(k)
        return carry
    lax.fori_loop(0, n, step, 0)


def unrolled(n, fn):
    if n > 8:
        return each(n, fn)
    for k in range(n):
        fn(k)


def kernel(
    n_pts, n_ctr, panels, chunk, sub,
    pts_hbm, cls_hbm, tgt_hbm, cw_hbm, inv_hbm, idx_hbm, cen_hbm, coef_hbm, fac_hbm, pinv_hbm,
    grad_ref, sol_ref,
    pts, cls, tgt, cw, inv_row, idx, head,
    cen, coef, pinv_raw, pinv, fac_raw, fac, rnorm, pnorm, pall, kmat, ksel,
    sel, total_acc, part, part_recv, wt_send, wt_recv, rsend, rbuf, rcount,
    wsend, wrecv, wcount, wsend_t, wrecv_t, tall, mixed, wpack, wblk, solsend, solrecv, rhssend, rhsrecv, acc,
    loc, cen_sem, pt_sem, fw_sem, pr_sem, wt_sem, rs_sem, w0_sem, w_sem, so_s, so_r, rh_s, rh_r,
):
    p_me, c_me = lax.axis_index("pts"), lax.axis_index("ctr")
    rows, feats = pts.shape
    group = rows * n_ctr
    centers = cen.shape[0]
    targets = tgt.shape[1]
    tcols = targets // n_pts
    own_rows, panel_rows = pinv.shape
    owners = panel_rows // own_rows
    my_panel = c_me // owners
    chunks = centers // chunk
    blocks = rbuf.shape[0]
    pt_blocks = blocks // n_pts
    per_block = n_ctr // pt_blocks
    width = rows * per_block
    me = p_me * n_ctr + c_me
    first_red = (n_ctr - blocks) // 2
    reduces = (c_me >= first_red) & (c_me < first_red + blocks)
    blk = jnp.where(reduces, c_me - first_red, 0)
    blk_pts = lax.rem(blk + p_me // 2 * 2, n_pts)
    own_block = reduces & (blk_pts == p_me)

    def remote(src, dst, send, recv, p, c):
        return pltpu.make_async_remote_copy(
            src_ref=src, dst_ref=dst, send_sem=send, recv_sem=recv,
            device_id={"pts": p, "ctr": c}, device_id_type=MESH,
        )

    def arrived(ref, sem):
        remote(ref, ref, sem.at[0], sem.at[1], p_me, lax.rem(c_me + 1, n_ctr)).wait_recv()

    def departed(ref, sem):
        remote(ref, ref, sem.at[0], sem.at[1], p_me, lax.rem(c_me + 1, n_ctr)).wait_send()

    def unless(flag, most, fn):
        @pl.when(flag)
        def _():
            fn(most - 1)

        @pl.when(jnp.logical_not(flag))
        def _():
            fn(most)

    def local(src, dst, k):
        return pltpu.make_async_copy(src, dst, loc.at[k])

    def cen_copy(k):
        at = pl.ds(pl.multiple_of(k * chunk, chunk), chunk)
        return pltpu.make_async_copy(cen_hbm.at[at], cen.at[at], cen_sem.at[k])

    pts_copy = local(pts_hbm, pts, 0)
    inv_copy = local(inv_hbm, inv_row, 1)
    cls_copy = local(cls_hbm, cls, 2)
    cw_copy = local(cw_hbm, cw, 3)
    tgt_copy = local(tgt_hbm, tgt, 4)
    idx_copy = local(idx_hbm, idx, 5)
    head_copy = local(idx_hbm.at[pl.ds(0, head.shape[0])], head, 6)
    coef_copy = local(coef_hbm, coef, 7)
    pinv_copy = local(pinv_hbm, pinv_raw, 8)
    fac_copy = local(fac_hbm.at[:, pl.ds(0, fac.shape[1])], fac_raw, 9)
    pts_copy.start()
    inv_copy.start()

    barrier = pltpu.get_barrier_semaphore()

    def peer(k):
        above = n_ctr - 1 - c_me
        low = jnp.where(k < above, n_ctr - 1 - k, k - above)
        high = jnp.where(k < c_me, k, n_ctr - 1 - k + c_me)
        return jnp.where(c_me < above, low, high)
    pair = p_me // 2 * 2

    def mate(k):
        return 2 * pair + 1 - p_me if k == 0 else lax.rem(pair + k + 1, n_pts)

    def greet(p, c):
        pl.semaphore_signal(barrier, inc=1, device_id={"pts": p, "ctr": c}, device_id_type=MESH)

    each(n_ctr - 1, lambda k: greet(p_me, peer(k)))
    for k in range(n_pts - 1):
        greet(mate(k), c_me)

    cls_copy.start()
    cw_copy.start()
    each(chunks, lambda k: cen_copy(k).start())
    idx_copy.start()
    tgt_copy.start()
    head_copy.start()
    coef_copy.start()

    pts_copy.wait()
    inv_copy.wait()
    inv = inv_row[...]
    own_slot = pl.ds(pl.multiple_of(me * rows, rows), rows)
    pall[own_slot, :] = (pts[...].astype(F32) * inv).astype(BF16)
    pl.semaphore_wait(barrier, n_ctr + n_pts - 2)

    def pt_copy(c_src, c_dst):
        slot = pl.ds(pl.multiple_of((p_me * n_ctr + c_src) * rows, rows), rows)
        return remote(pall.at[slot], pall.at[slot], pt_sem.at[0], pt_sem.at[1], p_me, c_dst)
    each(n_ctr - 1, lambda k: pt_copy(c_me, peer(k)).start())

    cls_copy.wait()
    cw_copy.wait()
    lane_of = lax.rem(c_me, per_block) * rows
    place = hot(iota((rows, width), 1) == iota((rows, width), 0) + lane_of)
    label = jnp.dot(
        jnp.broadcast_to(cls[...].astype(F32).astype(BF16), (8, rows)), place, preferred_element_type=F32
    )
    mine_lane = (iota((8, width), 1) >= lane_of) & (iota((8, width), 1) < lane_of + rows)
    weight = jnp.zeros((8, width), F32)
    for k in range(cw.shape[1]):
        weight = jnp.where(mine_lane & (label == float(k)), cw[0, k], weight)
    wt_send[...] = weight

    def wt_dest(k):
        return first_red + c_me // per_block * n_pts + k

    def wt_copy(c_src, c_dst):
        at = lax.rem(c_src, per_block)
        return remote(wt_send, wt_recv.at[at], wt_sem.at[0], wt_sem.at[1], p_me, c_dst)

    def not_me(c, fn):
        @pl.when(c != c_me)
        def _():
            fn(c)
    each(n_pts, lambda k: not_me(wt_dest(k), lambda c: wt_copy(c_me, c).start()))

    own_weights = reduces & (c_me // per_block == blk // n_pts)

    @pl.when(own_weights)
    def _():
        wt_recv[lax.rem(c_me, per_block)] = weight

    step = 256

    def scale(k):
        at = pl.ds(pl.multiple_of(k * step, step), step)
        scaled = (cen[at, :].astype(F32) * inv).astype(BF16)
        cen[at, :] = scaled
        rnorm[0:1, at] = half_norm_row(scaled)

    def scale_chunk(k):
        cen_copy(k).wait()
        unrolled(chunk // step, lambda j: scale(k * (chunk // step) + j))
    each(chunks, scale_chunk)

    idx_copy.wait()
    shift, wide_lanes = 64, idx.shape[1]
    per = wide_lanes // n_ctr
    slots = sel.shape[0]
    relative = idx[...] - c_me * centers
    relative = jnp.where((relative >= 0) & (relative < centers), relative, 0)
    fold = hot(iota((wide_lanes, wide_lanes), 0) // n_ctr == iota((wide_lanes, wide_lanes), 1))
    spread = hot(iota((slots, relative.shape[0]), 0) // per == iota((slots, relative.shape[0]), 1))

    def column(value):
        folded = jnp.dot(value.astype(F32).astype(BF16), fold, preferred_element_type=F32)
        return jnp.dot(spread, folded.astype(BF16), preferred_element_type=F32)
    both = shift * column(relative // shift) + column(lax.rem(relative, shift))
    at_lane = lax.rem(iota((slots, wide_lanes), 0), per) == iota((slots, wide_lanes), 1)
    local_row = jnp.sum(jnp.where(at_lane, both, 0.0), axis=1, keepdims=True).astype(jnp.int32)
    coef_copy.wait()
    tgt_copy.wait()
    head_copy.wait()
    pinv_copy.start()
    fac_copy.start()

    arrived(pall.at[pl.ds(0, (n_ctr - 1) * rows)], pt_sem)

    def group_at(p):
        return pl.ds(pl.multiple_of(p * group, group), group)

    def fw_copy(p_src, p_dst):
        at = group_at(p_src)
        return remote(pall.at[at], pall.at[at], fw_sem.at[0], fw_sem.at[1], p_dst, c_me)
    for k in range(n_pts - 1):
        fw_copy(p_me, mate(k)).start()

    def sub_at(k, j):
        return pl.ds(pl.multiple_of(k * chunk + j * sub, sub), sub)

    def kernel_block(left, norm, at):
        return jnp.exp(dot_nt(left, cen[at, :]) - norm - rnorm[0:1, at]).astype(BF16)
    mine = pall[group_at(p_me), :]
    mine_norm = half_norm(mine)
    pnorm[group_at(p_me), :] = jnp.broadcast_to(mine_norm, (group, LANES))
    total = jnp.zeros((group, targets), F32)
    saved = []
    for k in range(chunks):
        at = pl.ds(k * chunk, chunk)
        block = kernel_block(mine, mine_norm, at)
        kmat[group_at(p_me), at] = block
        if group > LANES:
            total = total + jnp.dot(block, coef[at, :], preferred_element_type=F32)
        else:
            saved.append((block, at))
    for block, at in saved:
        total = total + jnp.dot(block, coef[at, :], preferred_element_type=F32)
    total_acc[...] = total
    own_rows_at = pl.ds(pl.multiple_of(c_me * rows, rows), rows)
    total_acc[own_rows_at, :] = total_acc[own_rows_at, :] - tgt[...]
    for b in range(pt_blocks):
        turned = total_acc[b * width:(b + 1) * width, :].T
        for q in range(n_pts):
            part[b * n_pts + q] = turned[q * tcols:(q + 1) * tcols]

    def part_of(b):
        return b // n_pts * n_pts + lax.rem(b + p_me // 2 * 2, n_pts)

    def pr_copy(c_src, c_dst):
        return remote(
            part.at[part_of(c_dst - first_red)], part_recv.at[c_src], pr_sem.at[0], pr_sem.at[1], p_me, c_dst
        )
    def pr_dest(k):
        return jnp.where(c_me < n_ctr // 2, first_red + blocks - 1 - k, first_red + k)
    each(blocks, lambda k: not_me(pr_dest(k), lambda c: pr_copy(c_me, c).start()))
    part_recv[c_me] = part[part_of(blk)]

    sel[...] = jnp.zeros_like(sel)

    def select(k):
        at = pl.ds(pl.multiple_of(k * chunk, chunk), chunk)
        picked = hot(iota((slots, chunk), 1) == local_row - k * chunk)
        return jnp.dot(picked, cen[at, :], preferred_element_type=F32)
    sel[...] = functools.reduce(lambda a, k: a + select(k), range(1, chunks), select(0))

    arrived(pall.at[pl.ds(0, (n_pts - 1) * group)], fw_sem)

    def rs_slot(p, b):
        return p * pt_blocks + b

    def rs_copy(c_dst):
        at = rs_slot(p_me, blk // n_pts)
        return remote(rsend, rbuf.at[at], rs_sem.at[0], rs_sem.at[1], blk_pts, c_dst)

    @pl.when(reduces)
    def _():
        unless(own_weights, per_block, lambda n: arrived(wt_recv.at[pl.ds(0, n)], wt_sem))
        weights = jnp.sum(wt_recv[...], axis=0)[0:1]
        arrived(part_recv.at[pl.ds(0, n_ctr - 1)], pr_sem)
        residual = (weights * jnp.sum(part_recv[...], axis=0)).astype(BF16)
        rsend[...] = residual

        @pl.when(own_block)
        def _():
            rbuf[rs_slot(p_me, blk // n_pts)] = residual
            each(n_ctr - 1, lambda k: rs_copy(peer(k)).start())

        @pl.when(jnp.logical_not(own_block))
        def _():
            each(n_ctr - 1, lambda k: rs_copy(peer(k)).start())
            rs_copy(c_me).start()

    together = n_pts - 1 if group * n_pts <= 512 else 1
    for first in range(0, n_pts - 1, together):
        mates = [mate(k) for k in range(first, first + together)]
        left = jnp.concatenate([pall[group_at(p), :] for p in mates], axis=0)
        left_norm = half_norm(left)
        for k, p in enumerate(mates):
            pnorm[group_at(p), :] = jnp.broadcast_to(left_norm[k * group:(k + 1) * group], (group, LANES))

        def fill(k):
            for j in range(chunk // sub):
                at = sub_at(k, j)
                block = kernel_block(left, left_norm, at)
                for n, p in enumerate(mates):
                    kmat[group_at(p), at] = block[n * group:(n + 1) * group]
        unrolled(chunks, fill)

    chosen = sel[...].astype(BF16)
    chosen_norm = half_norm(chosen)
    span = 512

    def window_kernel(k):
        at = pl.ds(pl.multiple_of(k * span, span), span)
        norm = pnorm[at, :].T[0:1]
        ksel[:, at] = jnp.exp(dot_nt(chosen, pall[at, :]) - norm - chosen_norm).astype(BF16)
    each(pall.shape[0] // span, window_kernel)

    unless(own_block, blocks, lambda n: arrived(rbuf.at[pl.ds(0, n)], rs_sem))

    wide_t = jnp.concatenate([rbuf[b] for b in range(blocks)], axis=1)
    tall_t = jnp.concatenate([wide_t] * n_pts, axis=0)
    pieces, run = wsend.shape[1], wsend.shape[2]
    fine = pieces > 1
    lane_group = iota((run, targets), 1) // tcols
    per_panel = slots // panels

    def pack(panel):
        window = dot_nt(ksel[panel * per_panel:(panel + 1) * per_panel], tall_t)
        for g in range(pieces):
            packed = jnp.zeros((run, targets), F32)
            for h in range(n_pts):
                begin = (g * n_pts + h) * run
                packed = packed + jnp.where(lane_group == h, window[begin:begin + run], 0.0)
            wsend[panel, g] = packed.astype(BF16)
    own_piece = lax.rem(c_me, owners) * pieces // owners

    def w_first(d, c_dst):
        return remote(
            wsend.at[0, pl.ds(0, d + 1)], wrecv.at[c_me, pl.ds(0, d + 1)], w_sem.at[0], w_sem.at[1], p_me, c_dst
        )

    def w_later(c_dst):
        d = lax.rem(c_dst, owners) * pieces // owners
        return remote(
            wsend.at[c_dst // owners, pl.ds(d, 1)], wrecv.at[c_me, pl.ds(d, 1)], w_sem.at[0], w_sem.at[1], p_me, c_dst
        )
    alike = owners // pieces
    lane_parts = wsend_t.shape[0]

    def reach(d):
        return ((d + 1) * lane_parts + pieces - 1) // pieces

    def wt_first(d, c_src, c_dst):
        at = pl.ds(0, reach(d))
        return remote(wsend_t.at[at], wrecv_t.at[c_src, at], w0_sem.at[0], w0_sem.at[1 + c_src], p_me, c_dst)
    if fine:
        turned = dot_nt(wide_t, ksel[:per_panel]).astype(BF16)
        for g in range(lane_parts):
            wsend_t[g] = turned[:, g * LANES:(g + 1) * LANES]
    else:
        pack(0)
    for d in range(pieces):
        send = functools.partial(wt_first, d, c_me) if fine else functools.partial(w_first, d)
        each(alike, lambda j: not_me(d * alike + j, lambda c: send(c).start()))
    if fine:
        wrecv_t[c_me] = wsend_t[...]
    for panel in range(1, panels):
        pack(panel)
    each((panels - 1) * owners, lambda j: not_me(owners + j, lambda c: w_later(c).start()))
    if not fine:
        wrecv[c_me] = wsend[my_panel]
    else:
        @pl.when(my_panel > 0)
        def _():
            wrecv[c_me] = wsend[my_panel]

    def backward(k):
        at = pl.ds(pl.multiple_of(k * chunk, chunk), chunk)
        grad_ref[:, at] = jnp.dot(wide_t, kmat[:, at], preferred_element_type=F32)
    unrolled(chunks, backward)
    pinv_copy.wait()
    fac_copy.wait()
    if fine:
        @pl.when(my_panel > 0)
        def _():
            pinv[...] = pinv_raw[...].astype(BF16)

        @pl.when(my_panel == 0)
        def _():
            for g in range(own_rows // LANES):
                rows_at = slice(g * LANES, (g + 1) * LANES)
                for begin in range(0, panel_rows, LANES):
                    tall[g, begin:begin + LANES] = pinv_raw[rows_at, begin:begin + LANES].T
                for o in range(n_ctr):
                    mixed[o, :, rows_at] = tall[g, pl.ds(o, per_panel, stride=n_ctr), :].astype(BF16)
    else:
        pinv[...] = pinv_raw[...].astype(BF16)

    departed(pall.at[pl.ds(0, (n_ctr - 1) * rows)], pt_sem)
    unless(own_weights, n_pts, lambda n: departed(wt_recv.at[pl.ds(0, n)], wt_sem))
    departed(pall.at[pl.ds(0, (n_pts - 1) * group)], fw_sem)
    unless(reduces, blocks, lambda n: departed(part.at[pl.ds(0, n)], pr_sem))

    @pl.when(reduces)
    def _():
        unless(own_block, n_ctr, lambda n: departed(rcount.at[pl.ds(0, n)], rs_sem))

    w_ahead = sum((d + 1) * alike for d in range(pieces))
    w_after = (panels - 1) * owners

    def w_departed(own, panel):
        if fine:
            departed(rcount.at[pl.ds(0, sum(reach(d) for d in range(pieces)) - (reach(own) if panel == 0 else 0))], w0_sem)
            departed(wcount.at[pl.ds(0, w_after - (panel > 0))], w_sem)
        else:
            departed(wcount.at[pl.ds(0, w_ahead + w_after - (own + 1 if panel == 0 else 1))], w_sem)

    def unpack(g):
        for o in range(n_ctr):
            shard = head[o // wide_lanes, o % wide_lanes] // centers
            wpack[g, pl.ds(o, run, stride=n_ctr), :] = wrecv[shard, g].astype(F32)

    halves = solsend.shape[0]

    def so_copy(c_src, c_dst, h, late=0):
        at = c_src * halves + h
        return remote(solsend.at[h], solrecv.at[at], so_s.at[late], so_r.at[at], p_me, c_dst)

    def rh_copy(c_src, c_dst):
        at = lax.rem(c_src, owners)
        return remote(rhssend, rhsrecv.at[at], rh_s.at[lax.rem(c_dst, owners)], rh_r.at[at], p_me, c_dst)

    half_rows = own_rows // halves

    def send_solved(panel, h, result):
        sol_ref[:, h * half_rows:(h + 1) * half_rows] = result
        solsend[h] = result.astype(BF16)
        later = (panels - 1 - panel) * owners
        ahead = later // 2
        held = 1 if fine and later else 0
        each(ahead, lambda k: so_copy(c_me, (panel + 1) * owners + k, h).start())
        each(later - ahead - held, lambda k: so_copy(c_me, (panel + 1) * owners + ahead + k, h, 1).start())
        if held:
            departed_so(ahead, 0)

            @pl.when(c_me < owners // 2)
            def _():
                pl.delay(2500)
            so_copy(c_me, n_ctr - 1, h, 1).start()

    def departed_so(n, late):
        ref = solrecv.at[pl.ds(0, n * halves)]
        remote(ref, ref, so_s.at[late], so_r.at[0], p_me, lax.rem(c_me + 1, n_ctr)).wait_send()

    def departed_rest(n):
        if not fine:
            departed_so(n // 2, 0)
        departed_so(n - n // 2, 1)

    def first_panel(d):
        if fine:
            depth = reach(d) * LANES
            result = jnp.zeros((tcols, own_rows), F32)
            for k in range(n_ctr - 1, -1, -1):
                source = c_me if k == n_ctr - 1 else peer(k)
                if k < n_ctr - 1:
                    wt_first(d, source, source).wait_recv()
                spot = 0
                for o in range(1, n_ctr):
                    spot = jnp.where(head[o // wide_lanes, o % wide_lanes] // centers == source, o, spot)
                left = jnp.concatenate([wrecv_t[source, g] for g in range(reach(d))], axis=1)
                result = result + jnp.dot(left, mixed[spot, :depth], preferred_element_type=F32)
            send_solved(0, 0, result)
        else:
            arrived(wrecv.at[pl.ds(0, n_ctr - 1), pl.ds(0, d + 1)], w_sem)
            for g in range(d + 1):
                unpack(g)
            parts = []
            for g in range(d + 1):
                turned = wpack[g].T.astype(BF16)
                parts += [turned[h * tcols:(h + 1) * tcols] for h in range(n_pts)]
            rhs = jnp.concatenate(parts, axis=1)
            send_solved(0, 0, dot_nt(rhs, pinv[:, :(d + 1) * (panel_rows // pieces)]))
        if panels > 1:
            departed_rest((panels - 1) * owners)
        w_departed(d, 0)

    for d in range(pieces):
        @pl.when((my_panel == 0) & (own_piece == d))
        def _():
            first_panel(d)

    for panel in range(1, panels):
        @pl.when(my_panel == panel)
        def _():
            done = panel * owners
            position = c_me - done
            arrived(wrecv.at[pl.ds(0, n_ctr - 1), pl.ds(0, 1)], w_sem)
            fac[...] = fac_raw[...].astype(BF16)
            unpack(own_piece)
            if fine:
                turned = wpack[own_piece].T
                own = jnp.concatenate([turned[h * tcols:(h + 1) * tcols] for h in range(n_pts)], axis=1)
            else:
                offset = position * own_rows
                part_len = panel_rows // n_pts
                within = pl.multiple_of(lax.rem(offset, part_len), own_rows)
                turned = wpack[0, pl.ds(within, own_rows), :].T
                for g in range(n_pts):
                    wblk[g] = turned[g * tcols:(g + 1) * tcols]
                own = wblk[offset // part_len]
            if fine:
                for b in range(done):
                    for h in range(halves):
                        so_copy(b, b, h).wait_recv()
                        begin = b * own_rows + h * half_rows
                        own = own - dot_nt(solrecv[b * halves + h], fac[:, begin:begin + half_rows])
            else:
                each(done, lambda k: so_copy(k, k, 0).wait_recv())
                solved = jnp.concatenate([solrecv[b] for b in range(done)], axis=1)
                own = own - dot_nt(solved, fac[:, :done * own_rows])
            rhssend[...] = own.astype(BF16)

            def below(k, fn):
                @pl.when(k > position if fine else k != position)
                def _():
                    fn(done + k)
            each(owners, lambda k: below(k, lambda c: rh_copy(c_me, c).start()))
            if fine:
                acc[...] = jnp.zeros_like(acc)
                rhsrecv[position] = rhssend[...]
                for b in range(owners):
                    @pl.when(b <= position)
                    def _():
                        @pl.when(b < position)
                        def _():
                            rh_copy(done + b, done + b).wait_recv()
                        acc[...] += dot_nt(rhsrecv[b], pinv[:, b * own_rows:(b + 1) * own_rows])
                result = acc[...]
            else:
                rhsrecv[position] = rhssend[...]
                each(owners, lambda k: below(k, lambda c: rh_copy(c, c).wait_recv()))
                result = dot_nt(jnp.concatenate([rhsrecv[b] for b in range(owners)], axis=1), pinv[...])
            later = (panels - 1 - panel) * owners
            if later:
                for h in range(halves):
                    send_solved(panel, h, result[:, h * half_rows:(h + 1) * half_rows])
                departed_rest(later)
            else:
                sol_ref[...] = result
            each(owners, lambda k: below(k, lambda c: rh_copy(c_me, c).wait_send()))
            w_departed(0, panel)


def emit(grad_ref, sol_ref, grad_out, sol_out, sem):
    first = pltpu.make_async_copy(grad_ref, grad_out, sem.at[0])
    second = pltpu.make_async_copy(sol_ref, sol_out, sem.at[1])
    first.start()
    second.start()
    first.wait()
    second.wait()


def body(
    points, point_class, targets, class_weight, inv_scale, centers, coefficients, center_index, factor, panel_inverse
):
    n_pts, n_ctr = lax.axis_size("pts"), lax.axis_size("ctr")
    rows, feats = points.shape
    n_cen, n_tgt = coefficients.shape
    tcols = n_tgt // n_pts
    own_rows, panel_rows = panel_inverse.shape
    panels = factor.shape[1] // panel_rows
    owners = panel_rows // own_rows
    total = rows * n_pts * n_ctr
    group = rows * n_ctr
    per_block = LANES // rows
    pt_blocks = n_ctr // per_block
    blocks = n_pts * pt_blocks
    slots = center_index.shape[0] // n_ctr
    pieces = owners if own_rows % LANES == 0 else 1
    halves = 1
    lane_parts = max(1, slots // panels // LANES)
    run = slots // panels // pieces // n_pts
    w_most = pieces * (pieces + 1) // 2 * (owners // pieces) + (panels - 1) * owners
    solved_cols = panel_rows * (panels - 1)
    chunk = 1024
    index = center_index.reshape(-1, LANES)
    vmem = pl.BlockSpec(memory_space=pltpu.VMEM)
    hbm = pl.BlockSpec(memory_space=pltpu.HBM)
    dma = pltpu.SemaphoreType.DMA
    scratch = [
        pltpu.VMEM((rows, feats), BF16),
        pltpu.VMEM((1, rows), jnp.int32),
        pltpu.VMEM((rows, n_tgt), F32),
        pltpu.SMEM((1, class_weight.shape[0]), F32),
        pltpu.VMEM((1, feats), F32),
        pltpu.VMEM(index.shape, jnp.int32),
        pltpu.SMEM((8, LANES), jnp.int32),
        pltpu.VMEM((n_cen, feats), BF16),
        pltpu.VMEM((n_cen, n_tgt), BF16),
        pltpu.VMEM((own_rows, panel_rows), F32),
        pltpu.VMEM((own_rows, panel_rows), BF16),
        pltpu.VMEM((own_rows, solved_cols), F32),
        pltpu.VMEM((own_rows, solved_cols), BF16),
        pltpu.VMEM((8, n_cen), F32),
        pltpu.VMEM((total, LANES), F32),
        pltpu.VMEM((total, feats), BF16),
        pltpu.VMEM((total, n_cen), BF16),
        pltpu.VMEM((slots, total), BF16),
        pltpu.VMEM((slots, feats), F32),
        pltpu.VMEM((group, n_tgt), F32),
        pltpu.VMEM((blocks, tcols, LANES), F32),
        pltpu.VMEM((n_ctr, tcols, LANES), F32),
        pltpu.VMEM((8, LANES), F32),
        pltpu.VMEM((per_block, 8, LANES), F32),
        pltpu.VMEM((tcols, LANES), BF16),
        pltpu.VMEM((blocks, tcols, LANES), BF16),
        pltpu.VMEM((n_ctr, tcols, LANES), BF16),
        pltpu.VMEM((panels, pieces, run, n_tgt), BF16),
        pltpu.VMEM((n_ctr, pieces, run, n_tgt), BF16),
        pltpu.VMEM((w_most, run, n_tgt), BF16),
        pltpu.VMEM((lane_parts, tcols, LANES), BF16),
        pltpu.VMEM((n_ctr, lane_parts, tcols, LANES), BF16),
        pltpu.VMEM((max(1, own_rows // LANES), panel_rows, LANES), F32),
        pltpu.VMEM((n_ctr, slots // panels, own_rows), BF16),
        pltpu.VMEM((pieces, run * n_ctr, n_tgt), F32),
        pltpu.VMEM((n_pts, tcols, own_rows), F32),
        pltpu.VMEM((halves, tcols, own_rows // halves), BF16),
        pltpu.VMEM((owners * (panels - 1) * halves, tcols, own_rows // halves), BF16),
        pltpu.VMEM((tcols, own_rows), BF16),
        pltpu.VMEM((owners, tcols, own_rows), BF16),
        pltpu.VMEM((tcols, own_rows), F32),
        dma((10,)), dma((n_cen // chunk,)),
        dma((2,)), dma((2,)), dma((2,)), dma((2,)), dma((2,)), dma((1 + n_ctr,)), dma((2,)),
        dma((2,)), dma((owners * (panels - 1) * halves,)),
        dma((owners,)), dma((owners,)),
    ]
    grad, solved = pl.pallas_call(
        functools.partial(kernel, n_pts, n_ctr, panels, chunk, 512),
        out_shape=(
            pltpu.VMEM((tcols, n_cen), F32),
            pltpu.VMEM((tcols, own_rows), F32),
        ),
        in_specs=[hbm] * 10,
        out_specs=(vmem, vmem),
        scratch_shapes=scratch,
        compiler_params=pltpu.CompilerParams(
            collective_id=0, has_side_effects=True, vmem_limit_bytes=60000000
        ),
        name="falkon",
    )(
        points, point_class[None, :], targets, class_weight[None, :], inv_scale[None, :],
        index, centers, coefficients, factor, panel_inverse,
    )
    grad, solved = pl.pallas_call(
        emit,
        out_shape=(
            jax.ShapeDtypeStruct((tcols, n_cen), F32),
            jax.ShapeDtypeStruct((tcols, own_rows), F32),
        ),
        in_specs=[vmem, vmem],
        out_specs=(hbm, hbm),
        scratch_shapes=[dma((2,))],
        compiler_params=pltpu.CompilerParams(vmem_limit_bytes=1048576),
        name="emit",
    )(grad, solved)
    return grad.T, solved.T


def solution(mesh):
    placed = (
        P(("pts", "ctr"), None),
        P(("pts", "ctr")),
        P(("pts", "ctr"), None),
        P(),
        P(),
        P("ctr", None),
        P("ctr", None),
        P(),
        P("ctr", None),
        P("ctr", None),
    )
    return jax.shard_map(
        body,
        mesh=mesh,
        in_specs=placed,
        out_specs=(P("ctr", "pts"), P("ctr", "pts")),
        check_vma=False,
    )
```

```python
import functools

import jax
import jax.numpy as jnp
from jax import lax
from jax.experimental import pallas as pl
from jax.experimental.pallas import tpu as pltpu
from jax.sharding import PartitionSpec as P

MESH = pl.DeviceIdType.MESH
NT = (((1,), (1,)), ((), ()))
F32 = jnp.float32
BF16 = jnp.bfloat16
LANES = 128


def dot_nt(left, right):
    return lax.dot_general(left, right, NT, preferred_element_type=F32)


def iota(shape, dim):
    return lax.broadcasted_iota(jnp.int32, shape, dim)


def hot(mask):
    return jnp.where(mask, 1.0, 0.0).astype(BF16)


def half_norm(x):
    return 0.5 * jnp.sum(jnp.square(x.astype(F32)), axis=1, keepdims=True)


def half_norm_row(x):
    square = jnp.square(x.astype(F32))
    folded = square[:, :LANES]
    for begin in range(LANES, square.shape[1], LANES):
        folded = folded + square[:, begin:begin + LANES]
    return 0.5 * jnp.sum(folded.T, axis=0, keepdims=True)


def each(n, fn):
    def step(k, carry):
        fn(k)
        return carry
    lax.fori_loop(0, n, step, 0)


def unrolled(n, fn):
    if n > 8:
        return each(n, fn)
    for k in range(n):
        fn(k)


def kernel(
    n_pts, n_ctr, panels, chunk, sub,
    pts_hbm, cls_hbm, tgt_hbm, cw_hbm, inv_hbm, idx_hbm, cen_hbm, coef_hbm, fac_hbm, pinv_hbm,
    grad_ref, sol_ref,
    pts, cls, tgt, cw, inv_row, idx, head,
    cen, coef, pinv_raw, pinv, fac_raw, fac, rnorm, pnorm, pall, kmat, ksel,
    sel, total_acc, part, part_recv, wt_send, wt_recv, rsend, rbuf, rcount,
    wsend, wrecv, wcount, wsend_t, wrecv_t, tall, mixed, wpack, wblk, solsend, solrecv, rhssend, rhsrecv, acc,
    loc, cen_sem, pt_sem, fw_sem, pr_sem, wt_sem, rs_sem, w0_sem, w_sem, so_s, so_r, rh_s, rh_r,
):
    p_me, c_me = lax.axis_index("pts"), lax.axis_index("ctr")
    rows, feats = pts.shape
    group = rows * n_ctr
    centers = cen.shape[0]
    targets = tgt.shape[1]
    tcols = targets // n_pts
    own_rows, panel_rows = pinv.shape
    owners = panel_rows // own_rows
    my_panel = c_me // owners
    chunks = centers // chunk
    blocks = rbuf.shape[0]
    pt_blocks = blocks // n_pts
    per_block = n_ctr // pt_blocks
    width = rows * per_block
    me = p_me * n_ctr + c_me
    first_red = (n_ctr - blocks) // 2
    reduces = (c_me >= first_red) & (c_me < first_red + blocks)
    blk = jnp.where(reduces, c_me - first_red, 0)
    blk_pts = lax.rem(blk + p_me // 2 * 2, n_pts)
    own_block = reduces & (blk_pts == p_me)

    def remote(src, dst, send, recv, p, c):
        return pltpu.make_async_remote_copy(
            src_ref=src, dst_ref=dst, send_sem=send, recv_sem=recv,
            device_id={"pts": p, "ctr": c}, device_id_type=MESH,
        )

    def arrived(ref, sem):
        remote(ref, ref, sem.at[0], sem.at[1], p_me, lax.rem(c_me + 1, n_ctr)).wait_recv()

    def departed(ref, sem):
        remote(ref, ref, sem.at[0], sem.at[1], p_me, lax.rem(c_me + 1, n_ctr)).wait_send()

    def unless(flag, most, fn):
        @pl.when(flag)
        def _():
            fn(most - 1)

        @pl.when(jnp.logical_not(flag))
        def _():
            fn(most)

    def local(src, dst, k):
        return pltpu.make_async_copy(src, dst, loc.at[k])

    def cen_copy(k):
        at = pl.ds(pl.multiple_of(k * chunk, chunk), chunk)
        return pltpu.make_async_copy(cen_hbm.at[at], cen.at[at], cen_sem.at[k])

    pts_copy = local(pts_hbm, pts, 0)
    inv_copy = local(inv_hbm, inv_row, 1)
    cls_copy = local(cls_hbm, cls, 2)
    cw_copy = local(cw_hbm, cw, 3)
    tgt_copy = local(tgt_hbm, tgt, 4)
    idx_copy = local(idx_hbm, idx, 5)
    head_copy = local(idx_hbm.at[pl.ds(0, head.shape[0])], head, 6)
    coef_copy = local(coef_hbm, coef, 7)
    pinv_copy = local(pinv_hbm, pinv_raw, 8)
    fac_copy = local(fac_hbm.at[:, pl.ds(0, fac.shape[1])], fac_raw, 9)
    pts_copy.start()
    inv_copy.start()

    barrier = pltpu.get_barrier_semaphore()

    def peer(k):
        above = n_ctr - 1 - c_me
        low = jnp.where(k < above, n_ctr - 1 - k, k - above)
        high = jnp.where(k < c_me, k, n_ctr - 1 - k + c_me)
        return jnp.where(c_me < above, low, high)
    pair = p_me // 2 * 2

    def mate(k):
        return 2 * pair + 1 - p_me if k == 0 else lax.rem(pair + k + 1, n_pts)

    def greet(p, c):
        pl.semaphore_signal(barrier, inc=1, device_id={"pts": p, "ctr": c}, device_id_type=MESH)

    each(n_ctr - 1, lambda k: greet(p_me, peer(k)))
    for k in range(n_pts - 1):
        greet(mate(k), c_me)

    cls_copy.start()
    cw_copy.start()
    each(chunks, lambda k: cen_copy(k).start())
    idx_copy.start()
    tgt_copy.start()
    head_copy.start()
    coef_copy.start()

    pts_copy.wait()
    inv_copy.wait()
    inv = inv_row[...]
    own_slot = pl.ds(pl.multiple_of(me * rows, rows), rows)
    pall[own_slot, :] = (pts[...].astype(F32) * inv).astype(BF16)
    pl.semaphore_wait(barrier, n_ctr + n_pts - 2)

    def pt_copy(c_src, c_dst):
        slot = pl.ds(pl.multiple_of((p_me * n_ctr + c_src) * rows, rows), rows)
        return remote(pall.at[slot], pall.at[slot], pt_sem.at[0], pt_sem.at[1], p_me, c_dst)
    each(n_ctr - 1, lambda k: pt_copy(c_me, peer(k)).start())

    cls_copy.wait()
    cw_copy.wait()
    lane_of = lax.rem(c_me, per_block) * rows
    place = hot(iota((rows, width), 1) == iota((rows, width), 0) + lane_of)
    label = jnp.dot(
        jnp.broadcast_to(cls[...].astype(F32).astype(BF16), (8, rows)), place, preferred_element_type=F32
    )
    mine_lane = (iota((8, width), 1) >= lane_of) & (iota((8, width), 1) < lane_of + rows)
    weight = jnp.zeros((8, width), F32)
    for k in range(cw.shape[1]):
        weight = jnp.where(mine_lane & (label == float(k)), cw[0, k], weight)
    wt_send[...] = weight

    def wt_dest(k):
        return first_red + c_me // per_block * n_pts + k

    def wt_copy(c_src, c_dst):
        at = lax.rem(c_src, per_block)
        return remote(wt_send, wt_recv.at[at], wt_sem.at[0], wt_sem.at[1], p_me, c_dst)

    def not_me(c, fn):
        @pl.when(c != c_me)
        def _():
            fn(c)
    each(n_pts, lambda k: not_me(wt_dest(k), lambda c: wt_copy(c_me, c).start()))

    own_weights = reduces & (c_me // per_block == blk // n_pts)

    @pl.when(own_weights)
    def _():
        wt_recv[lax.rem(c_me, per_block)] = weight

    step = 256

    def scale(k):
        at = pl.ds(pl.multiple_of(k * step, step), step)
        scaled = (cen[at, :].astype(F32) * inv).astype(BF16)
        cen[at, :] = scaled
        rnorm[0:1, at] = half_norm_row(scaled)

    def scale_chunk(k):
        cen_copy(k).wait()
        unrolled(chunk // step, lambda j: scale(k * (chunk // step) + j))
    each(chunks, scale_chunk)

    idx_copy.wait()
    shift, wide_lanes = 64, idx.shape[1]
    per = wide_lanes // n_ctr
    slots = sel.shape[0]
    relative = idx[...] - c_me * centers
    relative = jnp.where((relative >= 0) & (relative < centers), relative, 0)
    fold = hot(iota((wide_lanes, wide_lanes), 0) // n_ctr == iota((wide_lanes, wide_lanes), 1))
    spread = hot(iota((slots, relative.shape[0]), 0) // per == iota((slots, relative.shape[0]), 1))

    def column(value):
        folded = jnp.dot(value.astype(F32).astype(BF16), fold, preferred_element_type=F32)
        return jnp.dot(spread, folded.astype(BF16), preferred_element_type=F32)
    both = shift * column(relative // shift) + column(lax.rem(relative, shift))
    at_lane = lax.rem(iota((slots, wide_lanes), 0), per) == iota((slots, wide_lanes), 1)
    local_row = jnp.sum(jnp.where(at_lane, both, 0.0), axis=1, keepdims=True).astype(jnp.int32)
    coef_copy.wait()
    tgt_copy.wait()
    head_copy.wait()
    pinv_copy.start()
    fac_copy.start()

    arrived(pall.at[pl.ds(0, (n_ctr - 1) * rows)], pt_sem)

    def group_at(p):
        return pl.ds(pl.multiple_of(p * group, group), group)

    def fw_copy(p_src, p_dst):
        at = group_at(p_src)
        return remote(pall.at[at], pall.at[at], fw_sem.at[0], fw_sem.at[1], p_dst, c_me)
    for k in range(n_pts - 1):
        fw_copy(p_me, mate(k)).start()

    def sub_at(k, j):
        return pl.ds(pl.multiple_of(k * chunk + j * sub, sub), sub)

    def kernel_block(left, norm, at):
        return jnp.exp(dot_nt(left, cen[at, :]) - norm - rnorm[0:1, at]).astype(BF16)
    mine = pall[group_at(p_me), :]
    mine_norm = half_norm(mine)
    pnorm[group_at(p_me), :] = jnp.broadcast_to(mine_norm, (group, LANES))
    total = jnp.zeros((group, targets), F32)
    saved = []
    for k in range(chunks):
        at = pl.ds(k * chunk, chunk)
        block = kernel_block(mine, mine_norm, at)
        kmat[group_at(p_me), at] = block
        if group > LANES:
            total = total + jnp.dot(block, coef[at, :], preferred_element_type=F32)
        else:
            saved.append((block, at))
    for block, at in saved:
        total = total + jnp.dot(block, coef[at, :], preferred_element_type=F32)
    total_acc[...] = total
    own_rows_at = pl.ds(pl.multiple_of(c_me * rows, rows), rows)
    total_acc[own_rows_at, :] = total_acc[own_rows_at, :] - tgt[...]
    for b in range(pt_blocks):
        turned = total_acc[b * width:(b + 1) * width, :].T
        for q in range(n_pts):
            part[b * n_pts + q] = turned[q * tcols:(q + 1) * tcols]

    def part_of(b):
        return b // n_pts * n_pts + lax.rem(b + p_me // 2 * 2, n_pts)

    def pr_copy(c_src, c_dst):
        return remote(
            part.at[part_of(c_dst - first_red)], part_recv.at[c_src], pr_sem.at[0], pr_sem.at[1], p_me, c_dst
        )
    def pr_dest(k):
        return jnp.where(c_me < n_ctr // 2, first_red + blocks - 1 - k, first_red + k)
    each(blocks, lambda k: not_me(pr_dest(k), lambda c: pr_copy(c_me, c).start()))
    part_recv[c_me] = part[part_of(blk)]

    sel[...] = jnp.zeros_like(sel)

    def select(k):
        at = pl.ds(pl.multiple_of(k * chunk, chunk), chunk)
        picked = hot(iota((slots, chunk), 1) == local_row - k * chunk)
        return jnp.dot(picked, cen[at, :], preferred_element_type=F32)
    sel[...] = functools.reduce(lambda a, k: a + select(k), range(1, chunks), select(0))

    arrived(pall.at[pl.ds(0, (n_pts - 1) * group)], fw_sem)

    def rs_slot(p, b):
        return p * pt_blocks + b

    def rs_copy(c_dst):
        at = rs_slot(p_me, blk // n_pts)
        return remote(rsend, rbuf.at[at], rs_sem.at[0], rs_sem.at[1], blk_pts, c_dst)

    @pl.when(reduces)
    def _():
        unless(own_weights, per_block, lambda n: arrived(wt_recv.at[pl.ds(0, n)], wt_sem))
        weights = jnp.sum(wt_recv[...], axis=0)[0:1]
        arrived(part_recv.at[pl.ds(0, n_ctr - 1)], pr_sem)
        residual = (weights * jnp.sum(part_recv[...], axis=0)).astype(BF16)
        rsend[...] = residual

        @pl.when(own_block)
        def _():
            rbuf[rs_slot(p_me, blk // n_pts)] = residual
            each(n_ctr - 1, lambda k: rs_copy(peer(k)).start())

        @pl.when(jnp.logical_not(own_block))
        def _():
            each(n_ctr - 1, lambda k: rs_copy(peer(k)).start())
            rs_copy(c_me).start()

    together = n_pts - 1 if group * n_pts <= 512 else 1
    for first in range(0, n_pts - 1, together):
        mates = [mate(k) for k in range(first, first + together)]
        left = jnp.concatenate([pall[group_at(p), :] for p in mates], axis=0)
        left_norm = half_norm(left)
        for k, p in enumerate(mates):
            pnorm[group_at(p), :] = jnp.broadcast_to(left_norm[k * group:(k + 1) * group], (group, LANES))

        def fill(k):
            for j in range(chunk // sub):
                at = sub_at(k, j)
                block = kernel_block(left, left_norm, at)
                for n, p in enumerate(mates):
                    kmat[group_at(p), at] = block[n * group:(n + 1) * group]
        unrolled(chunks, fill)

    chosen = sel[...].astype(BF16)
    chosen_norm = half_norm(chosen)
    span = 512

    def window_kernel(k):
        at = pl.ds(pl.multiple_of(k * span, span), span)
        norm = pnorm[at, :].T[0:1]
        ksel[:, at] = jnp.exp(dot_nt(chosen, pall[at, :]) - norm - chosen_norm).astype(BF16)
    each(pall.shape[0] // span, window_kernel)

    unless(own_block, blocks, lambda n: arrived(rbuf.at[pl.ds(0, n)], rs_sem))

    wide_t = jnp.concatenate([rbuf[b] for b in range(blocks)], axis=1)
    tall_t = jnp.concatenate([wide_t] * n_pts, axis=0)
    pieces, run = wsend.shape[1], wsend.shape[2]
    fine = pieces > 1
    lane_group = iota((run, targets), 1) // tcols
    per_panel = slots // panels

    def pack(panel):
        window = dot_nt(ksel[panel * per_panel:(panel + 1) * per_panel], tall_t)
        for g in range(pieces):
            packed = jnp.zeros((run, targets), F32)
            for h in range(n_pts):
                begin = (g * n_pts + h) * run
                packed = packed + jnp.where(lane_group == h, window[begin:begin + run], 0.0)
            wsend[panel, g] = packed.astype(BF16)
    own_piece = lax.rem(c_me, owners) * pieces // owners

    def w_first(d, c_dst):
        return remote(
            wsend.at[0, pl.ds(0, d + 1)], wrecv.at[c_me, pl.ds(0, d + 1)], w_sem.at[0], w_sem.at[1], p_me, c_dst
        )

    def w_later(c_dst):
        d = lax.rem(c_dst, owners) * pieces // owners
        return remote(
            wsend.at[c_dst // owners, pl.ds(d, 1)], wrecv.at[c_me, pl.ds(d, 1)], w_sem.at[0], w_sem.at[1], p_me, c_dst
        )
    alike = owners // pieces
    lane_parts = wsend_t.shape[0]

    def reach(d):
        return ((d + 1) * lane_parts + pieces - 1) // pieces

    def wt_first(d, c_src, c_dst):
        at = pl.ds(0, reach(d))
        return remote(wsend_t.at[at], wrecv_t.at[c_src, at], w0_sem.at[0], w0_sem.at[1 + c_src], p_me, c_dst)
    if fine:
        turned = dot_nt(wide_t, ksel[:per_panel]).astype(BF16)
        for g in range(lane_parts):
            wsend_t[g] = turned[:, g * LANES:(g + 1) * LANES]
    else:
        pack(0)
    for d in range(pieces):
        send = functools.partial(wt_first, d, c_me) if fine else functools.partial(w_first, d)
        each(alike, lambda j: not_me(d * alike + j, lambda c: send(c).start()))
    if fine:
        wrecv_t[c_me] = wsend_t[...]
    for panel in range(1, panels):
        pack(panel)
    each((panels - 1) * owners, lambda j: not_me(owners + j, lambda c: w_later(c).start()))
    if not fine:
        wrecv[c_me] = wsend[my_panel]
    else:
        @pl.when(my_panel > 0)
        def _():
            wrecv[c_me] = wsend[my_panel]

    def backward(k):
        at = pl.ds(pl.multiple_of(k * chunk, chunk), chunk)
        grad_ref[:, at] = jnp.dot(wide_t, kmat[:, at], preferred_element_type=F32)
    unrolled(chunks, backward)
    pinv_copy.wait()
    fac_copy.wait()
    if fine:
        @pl.when(my_panel > 0)
        def _():
            pinv[...] = pinv_raw[...].astype(BF16)

        @pl.when(my_panel == 0)
        def _():
            for g in range(own_rows // LANES):
                rows_at = slice(g * LANES, (g + 1) * LANES)
                for begin in range(0, panel_rows, LANES):
                    tall[g, begin:begin + LANES] = pinv_raw[rows_at, begin:begin + LANES].T
                for o in range(n_ctr):
                    mixed[o, :, rows_at] = tall[g, pl.ds(o, per_panel, stride=n_ctr), :].astype(BF16)
    else:
        pinv[...] = pinv_raw[...].astype(BF16)

    departed(pall.at[pl.ds(0, (n_ctr - 1) * rows)], pt_sem)
    unless(own_weights, n_pts, lambda n: departed(wt_recv.at[pl.ds(0, n)], wt_sem))
    departed(pall.at[pl.ds(0, (n_pts - 1) * group)], fw_sem)
    unless(reduces, blocks, lambda n: departed(part.at[pl.ds(0, n)], pr_sem))

    @pl.when(reduces)
    def _():
        unless(own_block, n_ctr, lambda n: departed(rcount.at[pl.ds(0, n)], rs_sem))

    w_ahead = sum((d + 1) * alike for d in range(pieces))
    w_after = (panels - 1) * owners

    def w_departed(own, panel):
        if fine:
            departed(rcount.at[pl.ds(0, sum(reach(d) for d in range(pieces)) - (reach(own) if panel == 0 else 0))], w0_sem)
            departed(wcount.at[pl.ds(0, w_after - (panel > 0))], w_sem)
        else:
            departed(wcount.at[pl.ds(0, w_ahead + w_after - (own + 1 if panel == 0 else 1))], w_sem)

    def unpack(g):
        for o in range(n_ctr):
            shard = head[o // wide_lanes, o % wide_lanes] // centers
            wpack[g, pl.ds(o, run, stride=n_ctr), :] = wrecv[shard, g].astype(F32)

    halves = solsend.shape[0]

    def so_copy(c_src, c_dst, h, late=0):
        at = c_src * halves + h
        return remote(solsend.at[h], solrecv.at[at], so_s.at[late], so_r.at[at], p_me, c_dst)

    def rh_copy(c_src, c_dst):
        at = lax.rem(c_src, owners)
        return remote(rhssend, rhsrecv.at[at], rh_s.at[lax.rem(c_dst, owners)], rh_r.at[at], p_me, c_dst)

    half_rows = own_rows // halves

    def send_solved(panel, h, result):
        sol_ref[:, h * half_rows:(h + 1) * half_rows] = result
        solsend[h] = result.astype(BF16)
        later = (panels - 1 - panel) * owners
        ahead = later // 2
        held = 1 if fine and later else 0
        each(ahead, lambda k: so_copy(c_me, (panel + 1) * owners + k, h).start())
        each(later - ahead - held, lambda k: so_copy(c_me, (panel + 1) * owners + ahead + k, h, 1).start())
        if held:
            departed_so(ahead, 0)

            @pl.when(c_me < owners // 2)
            def _():
                pl.delay(2500)
            so_copy(c_me, n_ctr - 1, h, 1).start()

    def departed_so(n, late):
        ref = solrecv.at[pl.ds(0, n * halves)]
        remote(ref, ref, so_s.at[late], so_r.at[0], p_me, lax.rem(c_me + 1, n_ctr)).wait_send()

    def departed_rest(n):
        if not fine:
            departed_so(n // 2, 0)
        departed_so(n - n // 2, 1)

    def first_panel(d):
        if fine:
            depth = reach(d) * LANES
            result = jnp.zeros((tcols, own_rows), F32)
            for k in range(n_ctr - 1, -1, -1):
                source = c_me if k == n_ctr - 1 else peer(k)
                if k < n_ctr - 1:
                    wt_first(d, source, source).wait_recv()
                spot = 0
                for o in range(1, n_ctr):
                    spot = jnp.where(head[o // wide_lanes, o % wide_lanes] // centers == source, o, spot)
                left = jnp.concatenate([wrecv_t[source, g] for g in range(reach(d))], axis=1)
                result = result + jnp.dot(left, mixed[spot, :depth], preferred_element_type=F32)
            send_solved(0, 0, result)
        else:
            arrived(wrecv.at[pl.ds(0, n_ctr - 1), pl.ds(0, d + 1)], w_sem)
            for g in range(d + 1):
                unpack(g)
            parts = []
            for g in range(d + 1):
                turned = wpack[g].T.astype(BF16)
                parts += [turned[h * tcols:(h + 1) * tcols] for h in range(n_pts)]
            rhs = jnp.concatenate(parts, axis=1)
            send_solved(0, 0, dot_nt(rhs, pinv[:, :(d + 1) * (panel_rows // pieces)]))
        if panels > 1:
            departed_rest((panels - 1) * owners)
        w_departed(d, 0)

    for d in range(pieces):
        @pl.when((my_panel == 0) & (own_piece == d))
        def _():
            first_panel(d)

    for panel in range(1, panels):
        @pl.when(my_panel == panel)
        def _():
            done = panel * owners
            position = c_me - done
            arrived(wrecv.at[pl.ds(0, n_ctr - 1), pl.ds(0, 1)], w_sem)
            fac[...] = fac_raw[...].astype(BF16)
            unpack(own_piece)
            if fine:
                turned = wpack[own_piece].T
                own = jnp.concatenate([turned[h * tcols:(h + 1) * tcols] for h in range(n_pts)], axis=1)
            else:
                offset = position * own_rows
                part_len = panel_rows // n_pts
                within = pl.multiple_of(lax.rem(offset, part_len), own_rows)
                turned = wpack[0, pl.ds(within, own_rows), :].T
                for g in range(n_pts):
                    wblk[g] = turned[g * tcols:(g + 1) * tcols]
                own = wblk[offset // part_len]
            if fine:
                turn = jnp.where(c_me == n_ctr - 1, owners // 2, 0)
                for step in range(done):
                    b = lax.rem(step + turn, done)
                    for h in range(halves):
                        so_copy(b, b, h).wait_recv()
                        begin = pl.multiple_of(b * own_rows + h * half_rows, half_rows)
                        own = own - dot_nt(solrecv[b * halves + h], fac[:, pl.ds(begin, half_rows)])
            else:
                each(done, lambda k: so_copy(k, k, 0).wait_recv())
                solved = jnp.concatenate([solrecv[b] for b in range(done)], axis=1)
                own = own - dot_nt(solved, fac[:, :done * own_rows])
            rhssend[...] = own.astype(BF16)

            def below(k, fn):
                @pl.when(k > position if fine else k != position)
                def _():
                    fn(done + k)
            each(owners, lambda k: below(k, lambda c: rh_copy(c_me, c).start()))
            if fine:
                acc[...] = jnp.zeros_like(acc)
                rhsrecv[position] = rhssend[...]
                for b in range(owners):
                    @pl.when(b <= position)
                    def _():
                        @pl.when(b < position)
                        def _():
                            rh_copy(done + b, done + b).wait_recv()
                        acc[...] += dot_nt(rhsrecv[b], pinv[:, b * own_rows:(b + 1) * own_rows])
                result = acc[...]
            else:
                rhsrecv[position] = rhssend[...]
                each(owners, lambda k: below(k, lambda c: rh_copy(c, c).wait_recv()))
                result = dot_nt(jnp.concatenate([rhsrecv[b] for b in range(owners)], axis=1), pinv[...])
            later = (panels - 1 - panel) * owners
            if later:
                for h in range(halves):
                    send_solved(panel, h, result[:, h * half_rows:(h + 1) * half_rows])
                departed_rest(later)
            else:
                sol_ref[...] = result
            each(owners, lambda k: below(k, lambda c: rh_copy(c_me, c).wait_send()))
            w_departed(0, panel)


def emit(grad_ref, sol_ref, grad_out, sol_out, sem):
    first = pltpu.make_async_copy(grad_ref, grad_out, sem.at[0])
    second = pltpu.make_async_copy(sol_ref, sol_out, sem.at[1])
    first.start()
    second.start()
    first.wait()
    second.wait()


def body(
    points, point_class, targets, class_weight, inv_scale, centers, coefficients, center_index, factor, panel_inverse
):
    n_pts, n_ctr = lax.axis_size("pts"), lax.axis_size("ctr")
    rows, feats = points.shape
    n_cen, n_tgt = coefficients.shape
    tcols = n_tgt // n_pts
    own_rows, panel_rows = panel_inverse.shape
    panels = factor.shape[1] // panel_rows
    owners = panel_rows // own_rows
    total = rows * n_pts * n_ctr
    group = rows * n_ctr
    per_block = LANES // rows
    pt_blocks = n_ctr // per_block
    blocks = n_pts * pt_blocks
    slots = center_index.shape[0] // n_ctr
    pieces = owners if own_rows % LANES == 0 else 1
    halves = 1
    lane_parts = max(1, slots // panels // LANES)
    run = slots // panels // pieces // n_pts
    w_most = pieces * (pieces + 1) // 2 * (owners // pieces) + (panels - 1) * owners
    solved_cols = panel_rows * (panels - 1)
    chunk = 1024
    index = center_index.reshape(-1, LANES)
    vmem = pl.BlockSpec(memory_space=pltpu.VMEM)
    hbm = pl.BlockSpec(memory_space=pltpu.HBM)
    dma = pltpu.SemaphoreType.DMA
    scratch = [
        pltpu.VMEM((rows, feats), BF16),
        pltpu.VMEM((1, rows), jnp.int32),
        pltpu.VMEM((rows, n_tgt), F32),
        pltpu.SMEM((1, class_weight.shape[0]), F32),
        pltpu.VMEM((1, feats), F32),
        pltpu.VMEM(index.shape, jnp.int32),
        pltpu.SMEM((8, LANES), jnp.int32),
        pltpu.VMEM((n_cen, feats), BF16),
        pltpu.VMEM((n_cen, n_tgt), BF16),
        pltpu.VMEM((own_rows, panel_rows), F32),
        pltpu.VMEM((own_rows, panel_rows), BF16),
        pltpu.VMEM((own_rows, solved_cols), F32),
        pltpu.VMEM((own_rows, solved_cols), BF16),
        pltpu.VMEM((8, n_cen), F32),
        pltpu.VMEM((total, LANES), F32),
        pltpu.VMEM((total, feats), BF16),
        pltpu.VMEM((total, n_cen), BF16),
        pltpu.VMEM((slots, total), BF16),
        pltpu.VMEM((slots, feats), F32),
        pltpu.VMEM((group, n_tgt), F32),
        pltpu.VMEM((blocks, tcols, LANES), F32),
        pltpu.VMEM((n_ctr, tcols, LANES), F32),
        pltpu.VMEM((8, LANES), F32),
        pltpu.VMEM((per_block, 8, LANES), F32),
        pltpu.VMEM((tcols, LANES), BF16),
        pltpu.VMEM((blocks, tcols, LANES), BF16),
        pltpu.VMEM((n_ctr, tcols, LANES), BF16),
        pltpu.VMEM((panels, pieces, run, n_tgt), BF16),
        pltpu.VMEM((n_ctr, pieces, run, n_tgt), BF16),
        pltpu.VMEM((w_most, run, n_tgt), BF16),
        pltpu.VMEM((lane_parts, tcols, LANES), BF16),
        pltpu.VMEM((n_ctr, lane_parts, tcols, LANES), BF16),
        pltpu.VMEM((max(1, own_rows // LANES), panel_rows, LANES), F32),
        pltpu.VMEM((n_ctr, slots // panels, own_rows), BF16),
        pltpu.VMEM((pieces, run * n_ctr, n_tgt), F32),
        pltpu.VMEM((n_pts, tcols, own_rows), F32),
        pltpu.VMEM((halves, tcols, own_rows // halves), BF16),
        pltpu.VMEM((owners * (panels - 1) * halves, tcols, own_rows // halves), BF16),
        pltpu.VMEM((tcols, own_rows), BF16),
        pltpu.VMEM((owners, tcols, own_rows), BF16),
        pltpu.VMEM((tcols, own_rows), F32),
        dma((10,)), dma((n_cen // chunk,)),
        dma((2,)), dma((2,)), dma((2,)), dma((2,)), dma((2,)), dma((1 + n_ctr,)), dma((2,)),
        dma((2,)), dma((owners * (panels - 1) * halves,)),
        dma((owners,)), dma((owners,)),
    ]
    grad, solved = pl.pallas_call(
        functools.partial(kernel, n_pts, n_ctr, panels, chunk, 512),
        out_shape=(
            pltpu.VMEM((tcols, n_cen), F32),
            pltpu.VMEM((tcols, own_rows), F32),
        ),
        in_specs=[hbm] * 10,
        out_specs=(vmem, vmem),
        scratch_shapes=scratch,
        compiler_params=pltpu.CompilerParams(
            collective_id=0, has_side_effects=True, vmem_limit_bytes=60000000
        ),
        name="falkon",
    )(
        points, point_class[None, :], targets, class_weight[None, :], inv_scale[None, :],
        index, centers, coefficients, factor, panel_inverse,
    )
    grad, solved = pl.pallas_call(
        emit,
        out_shape=(
            jax.ShapeDtypeStruct((tcols, n_cen), F32),
            jax.ShapeDtypeStruct((tcols, own_rows), F32),
        ),
        in_specs=[vmem, vmem],
        out_specs=(hbm, hbm),
        scratch_shapes=[dma((2,))],
        compiler_params=pltpu.CompilerParams(vmem_limit_bytes=1048576),
        name="emit",
    )(grad, solved)
    return grad.T, solved.T


def solution(mesh):
    placed = (
        P(("pts", "ctr"), None),
        P(("pts", "ctr")),
        P(("pts", "ctr"), None),
        P(),
        P(),
        P("ctr", None),
        P("ctr", None),
        P(),
        P("ctr", None),
        P("ctr", None),
    )
    return jax.shard_map(
        body,
        mesh=mesh,
        in_specs=placed,
        out_specs=(P("ctr", "pts"), P("ctr", "pts")),
        check_vma=False,
    )
```
